32 devices in a mesh: mz: 4 (over z), px: 8 (over y, x, core).
Axes of the slice: x: 2, y: 2, z: 4, core: 2. Of those that a mesh axis runs over, the one named last changes fastest.
Arguments:
- spectra: float32 [3072, 12288], P('px', 'mz'), may hold values from 0 to 10
- w_factor: float32 [48, 3072], P(None, ('px', 'mz')), may hold values from 0.05 to 1
- h_factor: float32 [48, 12288], P(None, ('mz', 'px')), may hold values from 0.05 to 1
Outputs:
- w_final: float32 [48, 3072], P(None, ('px', 'mz'))
- h_final: float32 [48, 12288], P(None, ('mz', 'px'))
- misfit: float32 [3072], P(('px', 'mz'))
The draws below stay inside these ranges and needn't reach their ends.
All inputs are finite; a program needn't handle non-finite values.
Results may differ from the reference program's by a relative error of at most 0.0001.
Values sent between devices are 32-bit elements; how exact they have to be, the bound alone decides.
No kernel may reach another device: no remote copies, remote signals or barrier semaphores. Data moves between devices by JAX's collectives and lax.ppermute only.
A program may use at most 64 MiB of HBM per device.

```python
import math
import jax
import jax.numpy as jnp
from jax import lax

RANK = 48
MZBINS = 12288
PIX_DEV = 384
ITERS = 3
PIXELS = 3072


def block_levels(stream_key, extent, shards, smallest, high):
    level, own = 1.0, jax.random.fold_in(stream_key, 6)
    for position, blocks in shards:
        draws = jnp.exp(jax.random.uniform(jax.random.fold_in(own, position), (blocks,), jnp.float32, smallest / len(shards), high / len(shards)))
        level = level * jnp.repeat(draws, extent[position] // blocks).reshape([-1 if axis == position else 1 for axis in range(len(extent))])
    return level


def setup_inputs(seed: int = 0) -> dict:
    key_of = jax.random.split(jax.random.key(seed), 4)
    return {
        "spectra": jnp.clip(10.0 * jax.random.uniform(key_of[0], (PIXELS, MZBINS), jnp.float32) ** block_levels(key_of[0], (PIXELS, MZBINS), ((0, 8), (1, 4)), -0.2, 0.2), 0.0, 10.0),
        "w_factor": jnp.clip(jnp.exp(math.log(1.0) - 2.9957323 * jax.random.uniform(key_of[1], (RANK, PIXELS), jnp.float32) ** block_levels(key_of[1], (RANK, PIXELS), ((1, 32),), -0.2, 0.2)), 0.05, 1.0),
        "h_factor": jnp.clip(jnp.exp(math.log(1.0) - 2.9957323 * jax.random.uniform(key_of[2], (RANK, MZBINS), jnp.float32) ** block_levels(key_of[2], (RANK, MZBINS), ((1, 32),), -0.2, 0.2)), 0.05, 1.0),
    }


def matmul(left, right):
    return jnp.dot(left, right, preferred_element_type=jnp.float32, precision=lax.Precision.HIGHEST)


def reference(spectra, w_factor, h_factor):
    loadings = w_factor
    components = h_factor
    for iteration in range(ITERS):
        components = components * matmul(loadings, spectra) / matmul(matmul(loadings, loadings.T), components)
        loadings = loadings * matmul(components, spectra.T) / matmul(matmul(components, components.T), loadings)
    blocks = spectra.reshape(PIXELS // PIX_DEV, PIX_DEV, MZBINS)
    load_blocks = loadings.T.reshape(PIXELS // PIX_DEV, PIX_DEV, RANK)

    def block_error(pair):
        data, load = pair
        diff = data - matmul(load, components)
        return jnp.sum(diff * diff, axis=1)

    misfit = lax.map(block_error, (blocks, load_blocks)).reshape(PIXELS)
    return loadings, components, misfit
```

```python
import functools

import jax
import jax.numpy as jnp
from jax import lax
from jax.experimental import pallas as pl
from jax.experimental.pallas import tpu as pltpu
from jax.sharding import PartitionSpec as P

ITERS = 3
LANES = 128
SUBLANES = 8
F32 = jnp.float32
BF16 = jnp.bfloat16
NN = (((1,), (0,)), ((), ()))
NT = (((1,), (1,)), ((), ()))
TN = (((0,), (0,)), ((), ()))


def matmul(left, right):
    return jnp.dot(left, right, preferred_element_type=F32, precision=lax.Precision.HIGHEST)


def plain_device(spectra, w_piece, h_piece):
    def rows_of(piece):
        return lax.all_gather(piece, "mz", axis=1, tiled=True)

    w_block = rows_of(w_piece)
    for _ in range(ITERS):
        numerator = lax.psum_scatter(matmul(w_block, spectra), "px", scatter_dimension=1, tiled=True)
        gram_w = lax.psum(matmul(w_block, w_block.T), "px")
        h_piece = h_piece * numerator / matmul(gram_w, h_piece)
        h_block = lax.all_gather(h_piece, "px", axis=1, tiled=True)
        numerator = lax.psum_scatter(matmul(h_block, spectra.T), "mz", scatter_dimension=1, tiled=True)
        gram_h = lax.psum(matmul(h_block, h_block.T), "mz")
        w_piece = w_piece * numerator / matmul(gram_h, w_piece)
        w_block = rows_of(w_piece)
    difference = spectra - matmul(w_block.T, h_block)
    partial_error = jnp.sum(difference * difference, axis=1)
    misfit = lax.psum_scatter(partial_error, "mz", scatter_dimension=0, tiled=True)
    return (w_piece, h_piece, misfit)


def split(value):
    high = value.astype(BF16)
    return high, (value - high.astype(F32)).astype(BF16)


def exact(left, right, dims):
    return lax.dot_general(left, right, dims, precision=lax.Precision.HIGHEST, preferred_element_type=F32)


def fast(left, right, dims):
    return lax.dot_general(left, right, dims, preferred_element_type=F32)


def stacked(value):
    high, low = split(value)
    return jnp.concatenate([high, low], axis=0), high


def product(stack, high, s_high, s_low, dims):
    rows = high.shape[0]
    both = fast(stack, s_high, dims)
    return both[:rows] + both[rows:] + fast(high, s_low, dims)


def pack_gram(ref, gram):
    rank = gram.shape[0]
    ref[rank:, :] = jnp.zeros((SUBLANES, ref.shape[1]), F32)
    for group in range(rank // SUBLANES):
        rows = slice(group * SUBLANES, (group + 1) * SUBLANES)
        ref[rank:, group * rank : (group + 1) * rank] = gram[rows, :]


def unpack_gram(packed, rank):
    return jnp.concatenate(
        [packed[:, group * rank : (group + 1) * rank] for group in range(rank // SUBLANES)], axis=0
    )


def params(**more):
    return pltpu.CompilerParams(vmem_limit_bytes=32 << 20, **more)


def vmem(count):
    return [pl.BlockSpec(memory_space=pltpu.VMEM)] * count


def cost(flops, moved):
    return pl.CostEstimate(flops=int(flops), bytes_accessed=int(moved), transcendentals=0)


def split_kernel(s_ref, high_ref, low_ref):
    high_ref[...], low_ref[...] = split(s_ref[...])


def split_call(spectra):
    rows, columns = spectra.shape
    step = min(columns, 512)
    spec = pl.BlockSpec((rows, step), lambda i: (0, i))
    return pl.pallas_call(
        split_kernel,
        grid=(columns // step,),
        in_specs=[spec],
        out_specs=[spec, spec],
        out_shape=[jax.ShapeDtypeStruct((rows, columns), BF16)] * 2,
        compiler_params=params(),
        cost_estimate=cost(4 * rows * columns, 8 * rows * columns),
        name="split_spectra",
    )(spectra)


def bins_of(relative, width):
    block = jnp.bitwise_xor(lax.axis_index("px"), relative)
    return pl.ds(pl.multiple_of(block * width, LANES), width)


def scatter_kernel(relatives, width, w_ref, high_ref, low_ref, *outs):
    w = w_ref[...]
    rank = w.shape[0]
    stack, w_high = stacked(w)
    gram = product(stack, w_high, *split(w), NT)
    for relative, out in zip(relatives, outs):
        here = bins_of(relative, width)
        out[:rank, :] = product(stack, w_high, high_ref[:, here], low_ref[:, here], NN)
        pack_gram(out, gram)


def scatter_call(relatives, width, w_block, high, low):
    rank, pixels = w_block.shape
    count = len(relatives)
    return pl.pallas_call(
        functools.partial(scatter_kernel, relatives, width),
        in_specs=vmem(3),
        out_specs=vmem(count),
        out_shape=[jax.ShapeDtypeStruct((rank + SUBLANES, width), F32)] * count,
        compiler_params=params(),
        cost_estimate=cost(6 * rank * pixels * width * count, 4 * pixels * width * count),
        name="loadings_times_spectra",
    )(w_block, high, low)


def update_kernel(factor_ref, *refs):
    parts, out = refs[:-1], refs[-1]
    factor = factor_ref[...]
    rank = factor.shape[0]
    total = parts[0][...]
    for part in parts[1:]:
        total = total + part[...]
    gram = unpack_gram(total[rank:], rank)
    out[...] = factor * total[:rank] / exact(gram, factor, NN)


def update_call(factor, *parts):
    rank, width = factor.shape
    return pl.pallas_call(
        update_kernel,
        in_specs=vmem(1 + len(parts)),
        out_specs=pl.BlockSpec(memory_space=pltpu.VMEM),
        out_shape=jax.ShapeDtypeStruct((rank, width), F32),
        compiler_params=params(),
        cost_estimate=cost(12 * rank * rank * width, 4 * rank * width * (2 + len(parts))),
        name="update",
    )(factor, *parts)


def add_kernel(left_ref, right_ref, out_ref):
    out_ref[...] = left_ref[...] + right_ref[...]


def add_call(left, right):
    return pl.pallas_call(
        add_kernel,
        in_specs=vmem(2),
        out_specs=pl.BlockSpec(memory_space=pltpu.VMEM),
        out_shape=jax.ShapeDtypeStruct(left.shape, F32),
        compiler_params=params(),
        cost_estimate=cost(left.size, 12 * left.size),
        name="add",
    )(left, right)


def gather_kernel(relatives, carried, high_ref, low_ref, *refs):
    out = refs[-1]
    pieces = refs[: len(relatives)]
    rank, width = pieces[0].shape
    total, gram = None, None
    for relative, piece in zip(relatives, pieces):
        h = piece[...]
        stack, h_high = stacked(h)
        here = bins_of(relative, width)
        term = product(stack, h_high, high_ref[:, here], low_ref[:, here], NT)
        square = product(stack, h_high, *split(h), NT)
        total = term if total is None else total + term
        gram = square if gram is None else gram + square
    out[:rank, :] = total
    pack_gram(out, gram)
    if carried:
        out[...] += refs[len(relatives)][...]


def gather_call(relatives, pieces, high, low, before):
    rank, width = pieces[0].shape
    pixels = high.shape[0]
    extra = () if before is None else (before,)
    count = len(relatives)
    return pl.pallas_call(
        functools.partial(gather_kernel, relatives, before is not None),
        in_specs=vmem(2 + count + len(extra)),
        out_specs=pl.BlockSpec(memory_space=pltpu.VMEM),
        out_shape=jax.ShapeDtypeStruct((rank + SUBLANES, pixels), F32),
        compiler_params=params(),
        cost_estimate=cost(6 * rank * pixels * width * count, 4 * pixels * width * count),
        name="spectra_times_components",
    )(high, low, *pieces, *extra)


def final_gather_kernel(relatives, groups, first, last, s_ref, w_ref, *refs):
    pieces, refs = refs[: len(relatives)], refs[len(relatives) :]
    if not first:
        before_ref, gram_before_ref, refs = refs[0], refs[1], refs[2:]
    rank, width = pieces[0].shape
    pixels = w_ref.shape[1]
    w_t = w_ref[...].T
    w0, w1 = split(w_t)
    w2 = (w_t - w0.astype(F32) - w1.astype(F32)).astype(BF16)
    left = jnp.concatenate([w0, w0, w1, w1, w0, w2], axis=1)
    lane = lax.broadcasted_iota(jnp.int32, (pixels, LANES), 1)
    zeros = functools.partial(jnp.zeros, dtype=BF16)
    total, gram = None, None
    for relative, piece in zip(relatives, pieces):
        h = piece[...]
        h0, h1 = split(h)
        h2 = (h - h0.astype(F32) - h1.astype(F32)).astype(BF16)
        s = s_ref[:, bins_of(relative, width)]
        right = jnp.concatenate([h0, h1, h0, h1, h2, h0], axis=0)
        d = s - fast(left, right, NN)
        tail = zeros((LANES - rank, width))
        tail2 = zeros((LANES - 2 * rank, width))
        pad = zeros((rank, width))
        num_high = jnp.concatenate([h0, tail], axis=0)
        num_both = jnp.concatenate([num_high, h1, tail], axis=0)
        err_high = jnp.concatenate([pad, h0, tail2], axis=0)
        err_both = jnp.concatenate([err_high, pad, h1, tail2], axis=0)
        s0, s1 = split(s)
        d0, d1 = split(d)
        both = fast(s0, num_both, NT) + fast(d0, err_both, NT)
        term = both[:, :LANES] + both[:, LANES:] + fast(s1, num_high, NT) + fast(d1, err_high, NT)
        squares = jnp.sum(d * d, axis=1, keepdims=True)
        term = jnp.where(lane == 2 * rank, squares, term)
        stack, h_high = stacked(h)
        square = product(stack, h_high, h0, h1, NT)
        total = term if total is None else total + term
        gram = square if gram is None else gram + square
    if not first:
        total = total + before_ref[...]
        gram = gram + gram_before_ref[...]
    if not last:
        refs[0][...] = total
        refs[1][...] = gram
        return
    outs, own_ref, scratch, w_scratch = refs[:groups], refs[groups], refs[-2], refs[-1]
    scratch[...] = total
    w_scratch[...] = w_t
    rows = pixels // groups
    me = lax.axis_index("mz")
    for relative, out in enumerate(outs):
        group = jnp.bitwise_xor(me, relative)
        out[:rows, :] = scratch[pl.ds(pl.multiple_of(group * rows, SUBLANES), rows), :]
        out[rows:, :] = jnp.zeros((rank, LANES), F32)
        out[rows:, :rank] = gram
    own_ref[...] = w_scratch[pl.ds(pl.multiple_of(me * rows, SUBLANES), rows), :]


def final_gather_call(relatives, groups, pieces, spectra, w_block, before, last):
    rank, width = pieces[0].shape
    pixels = w_block.shape[1]
    rows = pixels // groups
    count = len(relatives)
    first = before is None
    extra = () if first else tuple(before)
    if last:
        shapes = [jax.ShapeDtypeStruct((rows + rank, LANES), F32)] * groups
        shapes.append(jax.ShapeDtypeStruct((rows, rank), F32))
        scratch = [pltpu.VMEM((pixels, LANES), F32), pltpu.VMEM((pixels, rank), F32)]
    else:
        shapes = [jax.ShapeDtypeStruct((pixels, LANES), F32), jax.ShapeDtypeStruct((rank, rank), F32)]
        scratch = []
    return pl.pallas_call(
        functools.partial(final_gather_kernel, relatives, groups, first, last),
        in_specs=vmem(2 + count + len(extra)),
        out_specs=vmem(len(shapes)),
        out_shape=shapes,
        scratch_shapes=scratch,
        compiler_params=params(),
        cost_estimate=cost(24 * rank * pixels * width * count, 8 * pixels * width * count),
        name="final_products",
    )(spectra, w_block, *pieces, *extra)


def final_kernel(w_t_ref, *refs):
    parts, (w_out, misfit_out) = refs[:-2], refs[-2:]
    w_t = w_t_ref[...]
    rows, rank = w_t.shape
    total = parts[0][...]
    for part in parts[1:]:
        total = total + part[...]
    gram = total[rows:, :rank]
    num, err = total[:rows, :rank], total[:rows, rank : 2 * rank]
    new = w_t * num / exact(w_t, gram, NN)
    w_out[...] = new.T
    step = new - w_t
    change = step * (exact(step, gram, NN) - 2.0 * err)
    pick = (lax.broadcasted_iota(jnp.int32, (SUBLANES, LANES), 1) == 2 * rank).astype(F32)
    misfit = exact(pick, total[:rows], NT) + exact(jnp.ones((SUBLANES, rank), F32), change, NT)
    misfit_out[...] = misfit[:1]


def final_call(w_t, *parts):
    rows, rank = w_t.shape
    return pl.pallas_call(
        final_kernel,
        in_specs=vmem(1 + len(parts)),
        out_specs=vmem(2),
        out_shape=[jax.ShapeDtypeStruct((rank, rows), F32), jax.ShapeDtypeStruct((1, rows), F32)],
        compiler_params=params(),
        cost_estimate=cost(24 * rank * rank * rows, 4 * rows * LANES * len(parts)),
        name="final_update",
    )(w_t, *parts)


def join_kernel(*refs):
    pieces, out = refs[:-1], refs[-1]
    rank, width = pieces[0].shape
    whole = jnp.concatenate([piece[...] for piece in pieces], axis=1)
    out[...] = pltpu.roll(whole, lax.axis_index("mz") * width, 1)


def join_call(*pieces):
    rank, width = pieces[0].shape
    return pl.pallas_call(
        join_kernel,
        in_specs=vmem(len(pieces)),
        out_specs=pl.BlockSpec(memory_space=pltpu.VMEM),
        out_shape=jax.ShapeDtypeStruct((rank, width * len(pieces)), F32),
        compiler_params=params(),
        cost_estimate=cost(0, 8 * rank * width * len(pieces)),
        name="join",
    )(*pieces)


def swap(value, axis, size, mask):
    return lax.ppermute(value, axis, [(i, i ^ mask) for i in range(size)])


def fast_device(groups, owners, spectra, w_piece, h_piece):
    width = h_piece.shape[1]
    far = [r for r in range(owners - 1, 1, -1)]
    high, low = split_call(spectra)
    w_block = join_call(
        w_piece,
        *[
            lax.ppermute(w_piece, "mz", [(i, (i - k) % groups) for i in range(groups)])
            for k in range(1, groups)
        ],
    )
    evens = list(range(2, owners, 2))
    for iteration in range(ITERS):
        parts = scatter_call(far, width, w_block, high, low)
        sent = [swap(part, "px", owners, r) for part, r in zip(parts, far)]
        near = scatter_call([1, 0], width, w_block, high, low)
        sent.append(swap(near[0], "px", owners, 1))
        h_piece = update_call(h_piece, near[1], *sent)
        beside = swap(h_piece, "px", owners, 1)
        mine = [swap(h_piece, "px", owners, r) for r in evens]
        theirs = [swap(piece, "px", owners, 1) for piece in mine]
        odds = [r + 1 for r in evens]
        if iteration + 1 < ITERS:
            total = gather_call([0, 1], [h_piece, beside], high, low, None)
            total = gather_call(evens, mine, high, low, total)
            total = gather_call(odds, theirs, high, low, total)
            mask = 1
            while 2 * mask < groups:
                total = add_call(total, swap(total, "mz", groups, mask))
                mask *= 2
            w_block = update_call(w_block, total, swap(total, "mz", groups, mask))
        else:
            call = functools.partial(final_gather_call, spectra=spectra, w_block=w_block)
            total = call([0, 1], groups, [h_piece, beside], before=None, last=False)
            total = call(evens, groups, mine, before=total, last=False)
            *parts, w_t = call(odds, groups, theirs, before=total, last=True)
            sent = [swap(parts[k], "mz", groups, k) for k in range(1, groups)]
            w_final, misfit = final_call(w_t, parts[0], *sent)
    return w_final, h_piece, misfit.reshape(-1)


def per_device(groups, owners, spectra, w_piece, h_piece):
    rank = w_piece.shape[0]
    pixels, width = spectra.shape[0], h_piece.shape[1]

    def power(n):
        return n > 1 and n & (n - 1) == 0

    fits = (
        power(groups)
        and power(owners)
        and width % LANES == 0
        and pixels % LANES == 0
        and w_piece.shape[1] % SUBLANES == 0
        and rank % (2 * SUBLANES) == 0
        and rank // SUBLANES * rank <= min(width, pixels)
        and 2 * rank < LANES
    )
    if fits:
        return fast_device(groups, owners, spectra, w_piece, h_piece)
    return plain_device(spectra, w_piece, h_piece)


def solution(mesh):
    in_specs = (P("px", "mz"), P(None, ("px", "mz")), P(None, ("mz", "px")))
    out_specs = (P(None, ("px", "mz")), P(None, ("mz", "px")), P(("px", "mz")))
    body = functools.partial(per_device, mesh.shape["mz"], mesh.shape["px"])
    return jax.shard_map(body, mesh=mesh, in_specs=in_specs, out_specs=out_specs, check_vma=False)
```

```python
import functools

import jax
import jax.numpy as jnp
from jax import lax
from jax.experimental import pallas as pl
from jax.experimental.pallas import tpu as pltpu
from jax.sharding import PartitionSpec as P

ITERS = 3
LANES = 128
SUBLANES = 8
F32 = jnp.float32
BF16 = jnp.bfloat16
NN = (((1,), (0,)), ((), ()))
NT = (((1,), (1,)), ((), ()))
TN = (((0,), (0,)), ((), ()))


def matmul(left, right):
    return jnp.dot(left, right, preferred_element_type=F32, precision=lax.Precision.HIGHEST)


def plain_device(spectra, w_piece, h_piece):
    def rows_of(piece):
        return lax.all_gather(piece, "mz", axis=1, tiled=True)

    w_block = rows_of(w_piece)
    for _ in range(ITERS):
        numerator = lax.psum_scatter(matmul(w_block, spectra), "px", scatter_dimension=1, tiled=True)
        gram_w = lax.psum(matmul(w_block, w_block.T), "px")
        h_piece = h_piece * numerator / matmul(gram_w, h_piece)
        h_block = lax.all_gather(h_piece, "px", axis=1, tiled=True)
        numerator = lax.psum_scatter(matmul(h_block, spectra.T), "mz", scatter_dimension=1, tiled=True)
        gram_h = lax.psum(matmul(h_block, h_block.T), "mz")
        w_piece = w_piece * numerator / matmul(gram_h, w_piece)
        w_block = rows_of(w_piece)
    difference = spectra - matmul(w_block.T, h_block)
    partial_error = jnp.sum(difference * difference, axis=1)
    misfit = lax.psum_scatter(partial_error, "mz", scatter_dimension=0, tiled=True)
    return (w_piece, h_piece, misfit)


def split(value):
    high = value.astype(BF16)
    return high, (value - high.astype(F32)).astype(BF16)


def exact(left, right, dims):
    return lax.dot_general(left, right, dims, precision=lax.Precision.HIGHEST, preferred_element_type=F32)


def fast(left, right, dims):
    return lax.dot_general(left, right, dims, preferred_element_type=F32)


def stacked(value):
    high, low = split(value)
    return jnp.concatenate([high, low], axis=0), high


def product(stack, high, s_high, s_low, dims):
    rows = high.shape[0]
    both = fast(stack, s_high, dims)
    return both[:rows] + both[rows:] + fast(high, s_low, dims)


def pack_gram(ref, gram):
    rank = gram.shape[0]
    ref[rank:, :] = jnp.zeros((SUBLANES, ref.shape[1]), F32)
    for group in range(rank // SUBLANES):
        rows = slice(group * SUBLANES, (group + 1) * SUBLANES)
        ref[rank:, group * rank : (group + 1) * rank] = gram[rows, :]


def unpack_gram(packed, rank):
    return jnp.concatenate(
        [packed[:, group * rank : (group + 1) * rank] for group in range(rank // SUBLANES)], axis=0
    )


def params(mib=32):
    return pltpu.CompilerParams(vmem_limit_bytes=mib << 20)


def vmem(count):
    return [pl.BlockSpec(memory_space=pltpu.VMEM)] * count


def cost(flops, moved):
    return pl.CostEstimate(flops=int(flops), bytes_accessed=int(moved), transcendentals=0)


def split_kernel(step, s_ref, copy_ref, high_ref, low_ref, sems):
    columns = s_ref.shape[1]
    copies = []
    for index in range(columns // step):
        here = pl.ds(index * step, step)
        copies.append(pltpu.make_async_copy(s_ref.at[:, here], copy_ref.at[:, here], sems.at[index]))
        copies[-1].start()
    for index, copy in enumerate(copies):
        here = pl.ds(index * step, step)
        copy.wait()
        high_ref[:, here], low_ref[:, here] = split(copy_ref[:, here])


def split_call(spectra):
    rows, columns = spectra.shape
    step = columns // 8 if columns % (8 * LANES) == 0 else columns
    return pl.pallas_call(
        functools.partial(split_kernel, step),
        in_specs=[pl.BlockSpec(memory_space=pltpu.HBM)],
        out_specs=vmem(3),
        out_shape=[
            jax.ShapeDtypeStruct((rows, columns), F32),
            jax.ShapeDtypeStruct((rows, columns), BF16),
            jax.ShapeDtypeStruct((rows, columns), BF16),
        ],
        scratch_shapes=[pltpu.SemaphoreType.DMA((columns // step,))],
        compiler_params=params(44),
        cost_estimate=cost(4 * rows * columns, 12 * rows * columns),
        name="split_spectra",
    )(spectra)


def bins_of(relative, width):
    block = jnp.bitwise_xor(lax.axis_index("px"), relative)
    return pl.ds(pl.multiple_of(block * width, LANES), width)


def scatter_kernel(relatives, width, w_ref, high_ref, low_ref, out):
    w = w_ref[...]
    rank = w.shape[0]
    stack, w_high = stacked(w)
    gram = product(stack, w_high, *split(w), NT)
    for index, relative in enumerate(relatives):
        here = bins_of(relative, width)
        out[index, :rank, :] = product(stack, w_high, high_ref[:, here], low_ref[:, here], NN)
        pack_gram(out.at[index], gram)


def scatter_call(relatives, width, w_block, high, low):
    rank, pixels = w_block.shape
    count = len(relatives)
    return pl.pallas_call(
        functools.partial(scatter_kernel, relatives, width),
        in_specs=vmem(3),
        out_specs=pl.BlockSpec(memory_space=pltpu.VMEM),
        out_shape=jax.ShapeDtypeStruct((count, rank + SUBLANES, width), F32),
        compiler_params=params(),
        cost_estimate=cost(6 * rank * pixels * width * count, 4 * pixels * width * count),
        name="loadings_times_spectra",
    )(w_block, high, low)


def pair_kernel(own_ref, other_ref, *outs):
    for index, out in enumerate(outs):
        out[...] = own_ref[index + 1] + other_ref[index + 1]


def pair_call(own, other):
    count = own.shape[0] - 1
    return pl.pallas_call(
        pair_kernel,
        in_specs=vmem(2),
        out_specs=vmem(count),
        out_shape=[jax.ShapeDtypeStruct(own.shape[1:], F32)] * count,
        compiler_params=params(),
        cost_estimate=cost(own.size, 12 * own.size),
        name="pair_sums",
    )(own, other)


def update_kernel(stacks, factor_ref, *refs):
    parts, out = refs[:-1], refs[-1]
    factor = factor_ref[...]
    rank = factor.shape[0]
    total = None
    for index, part in enumerate(parts):
        value = part[0] if index < stacks else part[...]
        total = value if total is None else total + value
    gram = unpack_gram(total[rank:], rank)
    out[...] = factor * total[:rank] / exact(gram, factor, NN)


def update_call(factor, stacks, parts):
    rank, width = factor.shape
    parts = (*stacks, *parts)
    return pl.pallas_call(
        functools.partial(update_kernel, len(stacks)),
        in_specs=vmem(1 + len(parts)),
        out_specs=pl.BlockSpec(memory_space=pltpu.VMEM),
        out_shape=jax.ShapeDtypeStruct((rank, width), F32),
        compiler_params=params(),
        cost_estimate=cost(12 * rank * rank * width, 4 * rank * width * (2 + len(parts))),
        name="update",
    )(factor, *parts)


def add_kernel(left_ref, right_ref, out_ref):
    out_ref[...] = left_ref[...] + right_ref[...]


def add_call(left, right):
    return pl.pallas_call(
        add_kernel,
        in_specs=vmem(2),
        out_specs=pl.BlockSpec(memory_space=pltpu.VMEM),
        out_shape=jax.ShapeDtypeStruct(left.shape, F32),
        compiler_params=params(),
        cost_estimate=cost(left.size, 12 * left.size),
        name="add",
    )(left, right)


def gather_kernel(relatives, carried, high_ref, low_ref, *refs):
    out = refs[-1]
    pieces = refs[: len(relatives)]
    rank, width = pieces[0].shape
    total, gram = None, None
    for relative, piece in zip(relatives, pieces):
        h = piece[...]
        stack, h_high = stacked(h)
        here = bins_of(relative, width)
        term = product(stack, h_high, high_ref[:, here], low_ref[:, here], NT)
        square = product(stack, h_high, *split(h), NT)
        total = term if total is None else total + term
        gram = square if gram is None else gram + square
    out[:rank, :] = total
    pack_gram(out, gram)
    if carried:
        out[...] += refs[len(relatives)][...]


def gather_call(relatives, pieces, high, low, before):
    rank, width = pieces[0].shape
    pixels = high.shape[0]
    extra = () if before is None else (before,)
    count = len(relatives)
    return pl.pallas_call(
        functools.partial(gather_kernel, relatives, before is not None),
        in_specs=vmem(2 + count + len(extra)),
        out_specs=pl.BlockSpec(memory_space=pltpu.VMEM),
        out_shape=jax.ShapeDtypeStruct((rank + SUBLANES, pixels), F32),
        compiler_params=params(),
        cost_estimate=cost(6 * rank * pixels * width * count, 4 * pixels * width * count),
        name="spectra_times_components",
    )(high, low, *pieces, *extra)


def final_gather_kernel(relatives, groups, first, last, s_ref, w_ref, *refs):
    pieces, refs = refs[: len(relatives)], refs[len(relatives) :]
    if first:
        kept_ref = refs[-1]
        kept_ref[...] = pieces[0][...]
    else:
        before_ref, gram_before_ref, refs = refs[0], refs[1], refs[2:]
    rank, width = pieces[0].shape
    pixels = w_ref.shape[1]
    w_t = w_ref[...].T
    w0, w1 = split(w_t)
    w2 = (w_t - w0.astype(F32) - w1.astype(F32)).astype(BF16)
    left = jnp.concatenate([w0, w0, w1, w1, w0, w2], axis=1)
    lane = lax.broadcasted_iota(jnp.int32, (pixels, LANES), 1)
    half = LANES // 2
    zeros = functools.partial(jnp.zeros, dtype=BF16)
    total, gram = None, None
    for relative, piece in zip(relatives, pieces):
        h = piece[...]
        h0, h1 = split(h)
        h2 = (h - h0.astype(F32) - h1.astype(F32)).astype(BF16)
        right = jnp.concatenate([h0, h1, h0, h1, h2, h0], axis=0)
        d = s_ref[:, bins_of(relative, width)] - fast(left, right, NN)
        d0, d1 = split(d)
        tail = zeros((LANES - rank, width))
        high = jnp.concatenate([h0, tail], axis=0)
        both = fast(d0, jnp.concatenate([high, h1, tail], axis=0), NT)
        term = both[:, :LANES] + both[:, LANES:] + fast(d1, high, NT)
        squares = jnp.sum(d * d, axis=1, keepdims=True)
        term = jnp.where(lane == rank, squares, term)
        front = zeros((half, width))
        back = zeros((half - rank, width))
        stack = jnp.concatenate([h0, h1], axis=0)
        square = product(
            stack,
            h0,
            jnp.concatenate([front, h0, back], axis=0),
            jnp.concatenate([front, h1, back], axis=0),
            NT,
        )
        total = term if total is None else total + term
        gram = square if gram is None else gram + square
    if not first:
        total = total + before_ref[...]
        gram = gram + gram_before_ref[...]
    if not last:
        refs[0][...] = total
        refs[1][...] = gram
        return
    outs, own_ref, scratch, w_scratch = refs[:groups], refs[groups], refs[-2], refs[-1]
    scratch[...] = total
    w_scratch[...] = w_t
    rows = pixels // groups
    me = lax.axis_index("mz")
    for relative, out in enumerate(outs):
        group = jnp.bitwise_xor(me, relative)
        out[...] = scratch[pl.ds(pl.multiple_of(group * rows, SUBLANES), rows), :]
        out[:rank, :] += gram
    own_ref[...] = w_scratch[pl.ds(pl.multiple_of(me * rows, SUBLANES), rows), :]


def final_gather_call(relatives, groups, pieces, spectra, w_block, before, last):
    rank, width = pieces[0].shape
    pixels = w_block.shape[1]
    rows = pixels // groups
    count = len(relatives)
    first = before is None
    extra = () if first else tuple(before[:2])
    if last:
        shapes = [jax.ShapeDtypeStruct((rows, LANES), F32)] * groups
        shapes.append(jax.ShapeDtypeStruct((rows, rank), F32))
        scratch = [pltpu.VMEM((pixels, LANES), F32), pltpu.VMEM((pixels, rank), F32)]
    else:
        shapes = [jax.ShapeDtypeStruct((pixels, LANES), F32), jax.ShapeDtypeStruct((rank, LANES), F32)]
        scratch = []
    if first:
        shapes.append(jax.ShapeDtypeStruct((rank, width), F32))
    results = pl.pallas_call(
        functools.partial(final_gather_kernel, relatives, groups, first, last),
        in_specs=vmem(2 + count + len(extra)),
        out_specs=vmem(len(shapes)),
        out_shape=shapes,
        scratch_shapes=scratch,
        compiler_params=params(),
        cost_estimate=cost(24 * rank * pixels * width * count, 8 * pixels * width * count),
        name="final_products",
    )(spectra, w_block, *pieces, *extra)
    kept = () if first else (before[-1],)
    return (*results, *kept)


def final_kernel(w_t_ref, *refs):
    parts, (w_out, misfit_out) = refs[:-2], refs[-2:]
    w_t = w_t_ref[...]
    rows, rank = w_t.shape
    total = parts[0][...]
    for part in parts[1:]:
        total = total + part[...]
    gram = total[:rank, LANES // 2 : LANES // 2 + rank]
    err = total[:, :rank]
    den = exact(w_t, gram, NN)
    new = w_t * (err + den) / den
    w_out[...] = new.T
    step = new - w_t
    change = step * (exact(step, gram, NN) - 2.0 * err)
    pick = (lax.broadcasted_iota(jnp.int32, (SUBLANES, LANES), 1) == rank).astype(F32)
    misfit = exact(pick, total, NT) + exact(jnp.ones((SUBLANES, rank), F32), change, NT)
    misfit_out[...] = misfit[:1]


def final_call(w_t, *parts):
    rows, rank = w_t.shape
    return pl.pallas_call(
        final_kernel,
        in_specs=vmem(1 + len(parts)),
        out_specs=vmem(2),
        out_shape=[jax.ShapeDtypeStruct((rank, rows), F32), jax.ShapeDtypeStruct((1, rows), F32)],
        compiler_params=params(),
        cost_estimate=cost(24 * rank * rank * rows, 4 * rows * LANES * len(parts)),
        name="final_update",
    )(w_t, *parts)


def join_kernel(*refs):
    pieces, out = refs[:-1], refs[-1]
    rank, width = pieces[0].shape
    whole = jnp.concatenate([piece[...] for piece in pieces], axis=1)
    out[...] = pltpu.roll(whole, lax.axis_index("mz") * width, 1)


def join_call(*pieces):
    rank, width = pieces[0].shape
    return pl.pallas_call(
        join_kernel,
        in_specs=vmem(len(pieces)),
        out_specs=pl.BlockSpec(memory_space=pltpu.VMEM),
        out_shape=jax.ShapeDtypeStruct((rank, width * len(pieces)), F32),
        compiler_params=params(),
        cost_estimate=cost(0, 8 * rank * width * len(pieces)),
        name="join",
    )(*pieces)


def swap(value, axis, size, mask):
    return lax.ppermute(value, axis, [(i, i ^ mask) for i in range(size)])


def cross(value, groups, owners, even, odd):
    pairs = [
        (g * owners + o, (g ^ (odd if o % 2 else even)) * owners + o)
        for g in range(groups)
        for o in range(owners)
    ]
    return lax.ppermute(value, ("mz", "px"), pairs)


def spread(h_piece, owners, products):
    evens = list(range(owners - 2, 0, -2))
    beside = swap(h_piece, "px", owners, 1)
    mine = [swap(h_piece, "px", owners, r) for r in evens]
    total = products([0, 1], [h_piece, beside], None, False)
    theirs, held = [], []
    for index, (relative, piece) in enumerate(zip(evens, mine)):
        if index:
            piece, total = lax.optimization_barrier((piece, total))
        theirs.append(swap(piece, "px", owners, 1))
        held.append((relative, piece))
        if 0 < index < len(evens) - 1:
            total = products(*zip(*held), total, False)
            held = []
    held += [(r + 1, piece) for r, piece in zip(evens[:-1], theirs)]
    total = products(*zip(*held), total, False)
    return products([evens[-1] + 1], [theirs[-1]], total, True)


def fast_device(groups, owners, spectra, w_piece, h_piece):
    width = h_piece.shape[1]
    copy, high, low = split_call(spectra)
    w_block = join_call(
        w_piece,
        *[
            lax.ppermute(w_piece, "mz", [(i, (i - k) % groups) for i in range(groups)])
            for k in range(1, groups)
        ],
    )
    evens = list(range(owners - 2, 0, -2))
    masks = [1 << bit for bit in range(groups.bit_length() - 1)]
    for iteration in range(ITERS):
        theirs = scatter_call(list(range(1, owners, 2)), width, w_block, high, low)
        other = swap(theirs, "px", owners, 1)
        own = scatter_call(list(range(0, owners, 2)), width, w_block, high, low)
        sums = pair_call(own, other)
        sent = [swap(sums[r // 2 - 1], "px", owners, r) for r in evens]
        h_piece = update_call(h_piece, (own, other), sent)
        if iteration + 1 < ITERS:
            total = spread(
                h_piece,
                owners,
                lambda relatives, pieces, before, last: gather_call(relatives, pieces, high, low, before),
            )
            for even, odd in zip(masks[:-1], masks[:0:-1]):
                total = add_call(total, cross(total, groups, owners, even, odd))
            w_block = update_call(
                w_block, (), (total, cross(total, groups, owners, masks[-1], masks[0]))
            )
        else:
            parts = spread(
                h_piece,
                owners,
                lambda relatives, pieces, before, last: final_gather_call(
                    relatives, groups, pieces, copy, w_block, before, last
                ),
            )
            sent = [swap(parts[k], "mz", groups, k) for k in range(1, groups)]
            w_final, misfit = final_call(parts[groups], parts[0], *sent)
    return w_final, parts[-1], misfit.reshape(-1)


def per_device(groups, owners, spectra, w_piece, h_piece):
    rank = w_piece.shape[0]
    pixels, width = spectra.shape[0], h_piece.shape[1]

    def power(n):
        return n > 1 and n & (n - 1) == 0

    fits = (
        power(groups)
        and power(owners)
        and width % LANES == 0
        and pixels % LANES == 0
        and w_piece.shape[1] % SUBLANES == 0
        and rank % (2 * SUBLANES) == 0
        and rank // SUBLANES * rank <= min(width, pixels)
        and rank < LANES // 2
        and rank <= w_piece.shape[1]
    )
    if fits:
        return fast_device(groups, owners, spectra, w_piece, h_piece)
    return plain_device(spectra, w_piece, h_piece)


def solution(mesh):
    in_specs = (P("px", "mz"), P(None, ("px", "mz")), P(None, ("mz", "px")))
    out_specs = (P(None, ("px", "mz")), P(None, ("mz", "px")), P(("px", "mz")))
    body = functools.partial(per_device, mesh.shape["mz"], mesh.shape["px"])
    return jax.shard_map(body, mesh=mesh, in_specs=in_specs, out_specs=out_specs, check_vma=False)
```

```python
import functools

import jax
import jax.numpy as jnp
from jax import lax
from jax.experimental import pallas as pl
from jax.experimental.pallas import tpu as pltpu
from jax.sharding import PartitionSpec as P


ITERS = 3
LANES = 128
SUBLANES = 8
F32 = jnp.float32
BF16 = jnp.bfloat16
NN = (((1,), (0,)), ((), ()))
NT = (((1,), (1,)), ((), ()))


def matmul(left, right):
    return jnp.dot(left, right, preferred_element_type=F32, precision=lax.Precision.HIGHEST)


def plain_device(spectra, w_piece, h_piece):
    def rows_of(piece):
        return lax.all_gather(piece, "mz", axis=1, tiled=True)

    w_block = rows_of(w_piece)
    for _ in range(ITERS):
        numerator = lax.psum_scatter(matmul(w_block, spectra), "px", scatter_dimension=1, tiled=True)
        gram_w = lax.psum(matmul(w_block, w_block.T), "px")
        h_piece = h_piece * numerator / matmul(gram_w, h_piece)
        h_block = lax.all_gather(h_piece, "px", axis=1, tiled=True)
        numerator = lax.psum_scatter(matmul(h_block, spectra.T), "mz", scatter_dimension=1, tiled=True)
        gram_h = lax.psum(matmul(h_block, h_block.T), "mz")
        w_piece = w_piece * numerator / matmul(gram_h, w_piece)
        w_block = rows_of(w_piece)
    difference = spectra - matmul(w_block.T, h_block)
    partial_error = jnp.sum(difference * difference, axis=1)
    misfit = lax.psum_scatter(partial_error, "mz", scatter_dimension=0, tiled=True)
    return (w_piece, h_piece, misfit)


def split(value):
    high = value.astype(BF16)
    return high, (value - high.astype(F32)).astype(BF16)


def exact(left, right, dims):
    return lax.dot_general(left, right, dims, precision=lax.Precision.HIGHEST, preferred_element_type=F32)


def fast(left, right, dims):
    return lax.dot_general(left, right, dims, preferred_element_type=F32)


def stacked(value):
    high, low = split(value)
    return jnp.concatenate([high, low], axis=0), high


def product(stack, high, s_high, s_low, dims):
    rows = high.shape[0]
    both = fast(stack, s_high, dims)
    return both[:rows] + both[rows:] + fast(high, s_low, dims)


def pack_gram(ref, gram):
    rank = gram.shape[0]
    ref[rank:, :] = jnp.zeros((SUBLANES, ref.shape[1]), F32)
    for group in range(rank // SUBLANES):
        rows = slice(group * SUBLANES, (group + 1) * SUBLANES)
        ref[rank:, group * rank : (group + 1) * rank] = gram[rows, :]


def unpack_gram(packed, rank):
    return jnp.concatenate(
        [packed[:, group * rank : (group + 1) * rank] for group in range(rank // SUBLANES)], axis=0
    )


def params(mib=32):
    return pltpu.CompilerParams(vmem_limit_bytes=mib << 20)


def vmem(count):
    return [pl.BlockSpec(memory_space=pltpu.VMEM)] * count


def cost(flops, moved):
    return pl.CostEstimate(flops=int(flops), bytes_accessed=int(moved), transcendentals=0)


def split_kernel(step, s_ref, copy_ref, high_ref, low_ref, sems):
    columns = s_ref.shape[1]
    copies = []
    for index in range(columns // step):
        here = pl.ds(index * step, step)
        copies.append(pltpu.make_async_copy(s_ref.at[:, here], copy_ref.at[:, here], sems.at[index]))
        copies[-1].start()
    for index, copy in enumerate(copies):
        here = pl.ds(index * step, step)
        copy.wait()
        high_ref[:, here], low_ref[:, here] = split(copy_ref[:, here])


def split_call(spectra):
    rows, columns = spectra.shape
    step = columns // 8 if columns % (8 * LANES) == 0 else columns
    return pl.pallas_call(
        functools.partial(split_kernel, step),
        in_specs=[pl.BlockSpec(memory_space=pltpu.HBM)],
        out_specs=vmem(3),
        out_shape=[
            jax.ShapeDtypeStruct((rows, columns), F32),
            jax.ShapeDtypeStruct((rows, columns), BF16),
            jax.ShapeDtypeStruct((rows, columns), BF16),
        ],
        scratch_shapes=[pltpu.SemaphoreType.DMA((columns // step,))],
        compiler_params=params(44),
        cost_estimate=cost(4 * rows * columns, 12 * rows * columns),
        name="split_spectra",
    )(spectra)


def bins_of(relative, width):
    block = jnp.bitwise_xor(lax.axis_index("px"), relative)
    return pl.ds(pl.multiple_of(block * width, LANES), width)


def scatter_kernel(relatives, width, w_ref, high_ref, low_ref, out):
    w = w_ref[...]
    rank = w.shape[0]
    stack, w_high = stacked(w)
    gram = product(stack, w_high, *split(w), NT)
    for index, relative in enumerate(relatives):
        here = bins_of(relative, width)
        out[index, :rank, :] = product(stack, w_high, high_ref[:, here], low_ref[:, here], NN)
        pack_gram(out.at[index], gram)


def scatter_call(relatives, width, w_block, high, low):
    rank, pixels = w_block.shape
    count = len(relatives)
    return pl.pallas_call(
        functools.partial(scatter_kernel, relatives, width),
        in_specs=vmem(3),
        out_specs=pl.BlockSpec(memory_space=pltpu.VMEM),
        out_shape=jax.ShapeDtypeStruct((count, rank + SUBLANES, width), F32),
        compiler_params=params(),
        cost_estimate=cost(6 * rank * pixels * width * count, 4 * pixels * width * count),
        name="loadings_times_spectra",
    )(w_block, high, low)


def pair_kernel(own_ref, other_ref, *outs):
    for index, out in enumerate(outs):
        out[...] = own_ref[index + 1] + other_ref[index + 1]


def pair_call(own, other):
    count = own.shape[0] - 1
    return pl.pallas_call(
        pair_kernel,
        in_specs=vmem(2),
        out_specs=vmem(count),
        out_shape=[jax.ShapeDtypeStruct(own.shape[1:], F32)] * count,
        compiler_params=params(),
        cost_estimate=cost(own.size, 12 * own.size),
        name="pair_sums",
    )(own, other)


def update_kernel(stacks, factor_ref, *refs):
    parts, out = refs[:-1], refs[-1]
    factor = factor_ref[...]
    rank = factor.shape[0]
    total = None
    for index, part in enumerate(parts):
        value = part[0] if index < stacks else part[...]
        total = value if total is None else total + value
    gram = unpack_gram(total[rank:], rank)
    out[...] = factor * total[:rank] / exact(gram, factor, NN)


def update_call(factor, stacks, parts):
    rank, width = factor.shape
    parts = (*stacks, *parts)
    return pl.pallas_call(
        functools.partial(update_kernel, len(stacks)),
        in_specs=vmem(1 + len(parts)),
        out_specs=pl.BlockSpec(memory_space=pltpu.VMEM),
        out_shape=jax.ShapeDtypeStruct((rank, width), F32),
        compiler_params=params(),
        cost_estimate=cost(12 * rank * rank * width, 4 * rank * width * (2 + len(parts))),
        name="update",
    )(factor, *parts)


def add_kernel(left_ref, right_ref, out_ref):
    out_ref[...] = left_ref[...] + right_ref[...]


def add_call(left, right):
    return pl.pallas_call(
        add_kernel,
        in_specs=vmem(2),
        out_specs=pl.BlockSpec(memory_space=pltpu.VMEM),
        out_shape=jax.ShapeDtypeStruct(left.shape, F32),
        compiler_params=params(),
        cost_estimate=cost(left.size, 12 * left.size),
        name="add",
    )(left, right)


def gather_kernel(relatives, carried, high_ref, low_ref, *refs):
    out = refs[-1]
    pieces = refs[: len(relatives)]
    rank, width = pieces[0].shape
    total, gram = None, None
    for relative, piece in zip(relatives, pieces):
        h = piece[...]
        stack, h_high = stacked(h)
        here = bins_of(relative, width)
        term = product(stack, h_high, high_ref[:, here], low_ref[:, here], NT)
        square = product(stack, h_high, *split(h), NT)
        total = term if total is None else total + term
        gram = square if gram is None else gram + square
    out[:rank, :] = total
    pack_gram(out, gram)
    if carried:
        out[...] += refs[len(relatives)][...]


def gather_call(relatives, pieces, high, low, before):
    rank, width = pieces[0].shape
    pixels = high.shape[0]
    extra = () if before is None else (before,)
    count = len(relatives)
    return pl.pallas_call(
        functools.partial(gather_kernel, relatives, before is not None),
        in_specs=vmem(2 + count + len(extra)),
        out_specs=pl.BlockSpec(memory_space=pltpu.VMEM),
        out_shape=jax.ShapeDtypeStruct((rank + SUBLANES, pixels), F32),
        compiler_params=params(),
        cost_estimate=cost(6 * rank * pixels * width * count, 4 * pixels * width * count),
        name="spectra_times_components",
    )(high, low, *pieces, *extra)


def thirds(value):
    high, low = split(value)
    return high, low, (value - high.astype(F32) - low.astype(F32)).astype(BF16)


def final_gather_kernel(relatives, groups, first, last, s_ref, w_ref, *refs):
    pieces, refs = refs[: len(relatives)], refs[len(relatives) :]
    carried, refs = ((), refs) if first else (refs[:3], refs[3:])
    rank, width = pieces[0].shape
    pixels = w_ref.shape[1]
    w_t = w_ref[...].T
    w0, w1, w2 = thirds(w_t)
    left = jnp.concatenate([w0, w0, w1, w1, w2], axis=1)
    half = LANES // 2
    front = jnp.zeros((half, width), BF16)
    back = jnp.zeros((half - rank, width), BF16)
    sums = [ref[...] for ref in carried] if carried else [None] * 3
    for relative, piece in zip(relatives, pieces):
        h0, h1, _ = thirds(piece[...])
        right = jnp.concatenate([h0, h1, h0, h1, h0], axis=0)
        d = s_ref[:, bins_of(relative, width)] - fast(left, right, NN)
        stack = jnp.concatenate([h0, h1], axis=0)
        error = product(stack, h0, *split(d), NT)
        gram = product(
            stack,
            h0,
            jnp.concatenate([front, h0, back], axis=0),
            jnp.concatenate([front, h1, back], axis=0),
            NT,
        )
        square = d * d
        folded = square[:, :LANES]
        for start in range(LANES, width, LANES):
            folded = folded + square[:, start : start + LANES]
        terms = (error, folded, gram)
        sums = [t if s is None else s + t for s, t in zip(sums, terms)]
    error, folded, gram = sums
    if not last:
        for ref, value in zip(refs, sums):
            ref[...] = value
        return
    outs, own_ref, scratch, w_scratch = refs[:groups], refs[groups], refs[-2], refs[-1]
    tall = jnp.concatenate([error, jnp.zeros((LANES - rank, pixels), F32)], axis=0)
    lane = lax.broadcasted_iota(jnp.int32, (pixels, LANES), 1)
    scratch[...] = jnp.where(lane == rank, jnp.sum(folded, axis=1, keepdims=True), tall.T)
    w_scratch[...] = w_t
    rows = pixels // groups
    me = lax.axis_index("mz")
    for relative, out in enumerate(outs):
        group = jnp.bitwise_xor(me, relative)
        out[...] = scratch[pl.ds(pl.multiple_of(group * rows, SUBLANES), rows), :]
        out[:rank, :] += gram
    own_ref[...] = w_scratch[pl.ds(pl.multiple_of(me * rows, SUBLANES), rows), :]


def final_gather_call(relatives, groups, pieces, spectra, w_block, before, last):
    rank, width = pieces[0].shape
    pixels = w_block.shape[1]
    rows = pixels // groups
    count = len(relatives)
    first = before is None
    extra = () if first else tuple(before)
    shapes = [(rank, pixels), (pixels, LANES), (rank, LANES)]
    scratch = []
    if last:
        shapes = [(rows, LANES)] * groups + [(rows, rank)]
        scratch = [pltpu.VMEM((pixels, LANES), F32), pltpu.VMEM((pixels, rank), F32)]
    return pl.pallas_call(
        functools.partial(final_gather_kernel, relatives, groups, first, last),
        in_specs=vmem(2 + count + len(extra)),
        out_specs=vmem(len(shapes)),
        out_shape=[jax.ShapeDtypeStruct(shape, F32) for shape in shapes],
        scratch_shapes=scratch,
        compiler_params=params(),
        cost_estimate=cost(18 * rank * pixels * width * count, 8 * pixels * width * count),
        name="final_products",
    )(spectra, w_block, *pieces, *extra)


def final_kernel(w_t_ref, h_ref, *refs):
    parts, (w_out, h_out, misfit_out) = refs[:-3], refs[-3:]
    h_out[...] = h_ref[...]
    w_t = w_t_ref[...]
    _, rank = w_t.shape
    total = parts[0][...]
    for part in parts[1:]:
        total = total + part[...]
    gram = total[:rank, LANES // 2 : LANES // 2 + rank]
    err = total[:, :rank]
    den = exact(w_t, gram, NN)
    new = w_t * (err + den) / den
    w_out[...] = new.T
    step = new - w_t
    change = step * (exact(step, gram, NN) - 2.0 * err)
    pick = (lax.broadcasted_iota(jnp.int32, (SUBLANES, LANES), 1) == rank).astype(F32)
    misfit = exact(pick, total, NT) + exact(jnp.ones((SUBLANES, rank), F32), change, NT)
    misfit_out[...] = misfit[:1]


def final_call(w_t, h_piece, *parts):
    rows, rank = w_t.shape
    return pl.pallas_call(
        final_kernel,
        in_specs=vmem(2 + len(parts)),
        out_specs=vmem(3),
        out_shape=[
            jax.ShapeDtypeStruct((rank, rows), F32),
            jax.ShapeDtypeStruct(h_piece.shape, F32),
            jax.ShapeDtypeStruct((1, rows), F32),
        ],
        compiler_params=params(),
        cost_estimate=cost(24 * rank * rank * rows, 4 * rows * LANES * len(parts)),
        name="final_update",
    )(w_t, h_piece, *parts)


def join_kernel(*refs):
    pieces, out = refs[:-1], refs[-1]
    _, width = pieces[0].shape
    whole = jnp.concatenate([piece[...] for piece in pieces], axis=1)
    out[...] = pltpu.roll(whole, lax.axis_index("mz") * width, 1)


def join_call(*pieces):
    rank, width = pieces[0].shape
    return pl.pallas_call(
        join_kernel,
        in_specs=vmem(len(pieces)),
        out_specs=pl.BlockSpec(memory_space=pltpu.VMEM),
        out_shape=jax.ShapeDtypeStruct((rank, width * len(pieces)), F32),
        compiler_params=params(),
        cost_estimate=cost(0, 8 * rank * width * len(pieces)),
        name="join",
    )(*pieces)


def swap(value, axis, size, mask):
    return lax.ppermute(value, axis, [(i, i ^ mask) for i in range(size)])


def cross(value, groups, owners, even, odd):
    pairs = [
        (g * owners + o, (g ^ (even if o % 2 else odd)) * owners + o)
        for g in range(groups)
        for o in range(owners)
    ]
    return lax.ppermute(value, ("mz", "px"), pairs)


def spread(h_piece, owners, products):
    evens = [owners - 2, *range(2, owners - 2, 2)]
    mine = []
    for relative in evens:
        mine.append(swap(h_piece, "px", owners, relative))
    beside = swap(h_piece, "px", owners, 1)
    theirs = []
    for piece in mine:
        theirs.append(swap(piece, "px", owners, 1))
    total = products([0, 1], [h_piece, beside], None, False)
    total = products(evens, mine, total, False)
    return products([r + 1 for r in evens], theirs, total, True)


def fast_device(groups, owners, spectra, w_piece, h_piece):
    width = h_piece.shape[1]
    copy, high, low = split_call(spectra)
    w_block = join_call(
        w_piece,
        *[
            lax.ppermute(w_piece, "mz", [(i, (i - k) % groups) for i in range(groups)])
            for k in range(1, groups)
        ],
    )
    evens = list(range(owners - 2, 0, -2))
    masks = [1 << bit for bit in range(groups.bit_length() - 1)]
    for iteration in range(ITERS):
        theirs = scatter_call(list(range(1, owners, 2)), width, w_block, high, low)
        other = swap(theirs, "px", owners, 1)
        own = scatter_call(list(range(0, owners, 2)), width, w_block, high, low)
        sums = pair_call(own, other)
        sent = [swap(sums[r // 2 - 1], "px", owners, r) for r in evens]
        h_piece = update_call(h_piece, (own, other), sent)
        if iteration + 1 < ITERS:
            total = spread(
                h_piece,
                owners,
                lambda relatives, pieces, before, last: gather_call(relatives, pieces, high, low, before),
            )
            for even, odd in zip(masks[:-1], masks[:0:-1]):
                total = add_call(total, cross(total, groups, owners, even, odd))
            w_block = update_call(
                w_block, (), (total, cross(total, groups, owners, masks[-1], masks[0]))
            )
        else:
            parts = spread(
                h_piece,
                owners,
                lambda relatives, pieces, before, last: final_gather_call(
                    relatives, groups, pieces, copy, w_block, before, last
                ),
            )
            sent = [swap(parts[k], "mz", groups, k) for k in range(1, groups)]
            w_final, h_final, misfit = final_call(parts[groups], h_piece, parts[0], *sent)
    return w_final, h_final, misfit.reshape(-1)


def per_device(groups, owners, spectra, w_piece, h_piece):
    rank = w_piece.shape[0]
    pixels, width = spectra.shape[0], h_piece.shape[1]

    def power(n):
        return n > 1 and n & (n - 1) == 0

    fits = (
        power(groups)
        and power(owners)
        and width % LANES == 0
        and pixels % LANES == 0
        and w_piece.shape[1] % SUBLANES == 0
        and rank % (2 * SUBLANES) == 0
        and rank // SUBLANES * rank <= min(width, pixels)
        and rank < LANES // 2
        and rank <= w_piece.shape[1]
    )
    if fits:
        return fast_device(groups, owners, spectra, w_piece, h_piece)
    return plain_device(spectra, w_piece, h_piece)


def solution(mesh):
    in_specs = (P("px", "mz"), P(None, ("px", "mz")), P(None, ("mz", "px")))
    out_specs = (P(None, ("px", "mz")), P(None, ("mz", "px")), P(("px", "mz")))
    body = functools.partial(per_device, mesh.shape["mz"], mesh.shape["px"])
    return jax.shard_map(body, mesh=mesh, in_specs=in_specs, out_specs=out_specs, check_vma=False)
```

```python
import functools

import jax
import jax.numpy as jnp
from jax import lax
from jax.experimental import pallas as pl
from jax.experimental.pallas import tpu as pltpu
from jax.sharding import PartitionSpec as P


ITERS = 3
LANES = 128
SUBLANES = 8
F32 = jnp.float32
BF16 = jnp.bfloat16
NN = (((1,), (0,)), ((), ()))
NT = (((1,), (1,)), ((), ()))


def matmul(left, right):
    return jnp.dot(left, right, preferred_element_type=F32, precision=lax.Precision.HIGHEST)


def plain_device(spectra, w_piece, h_piece):
    def rows_of(piece):
        return lax.all_gather(piece, "mz", axis=1, tiled=True)

    w_block = rows_of(w_piece)
    for _ in range(ITERS):
        numerator = lax.psum_scatter(matmul(w_block, spectra), "px", scatter_dimension=1, tiled=True)
        gram_w = lax.psum(matmul(w_block, w_block.T), "px")
        h_piece = h_piece * numerator / matmul(gram_w, h_piece)
        h_block = lax.all_gather(h_piece, "px", axis=1, tiled=True)
        numerator = lax.psum_scatter(matmul(h_block, spectra.T), "mz", scatter_dimension=1, tiled=True)
        gram_h = lax.psum(matmul(h_block, h_block.T), "mz")
        w_piece = w_piece * numerator / matmul(gram_h, w_piece)
        w_block = rows_of(w_piece)
    difference = spectra - matmul(w_block.T, h_block)
    partial_error = jnp.sum(difference * difference, axis=1)
    misfit = lax.psum_scatter(partial_error, "mz", scatter_dimension=0, tiled=True)
    return (w_piece, h_piece, misfit)


def split(value):
    high = value.astype(BF16)
    return high, (value - high.astype(F32)).astype(BF16)


def exact(left, right, dims):
    return lax.dot_general(left, right, dims, precision=lax.Precision.HIGHEST, preferred_element_type=F32)


def fast(left, right, dims):
    return lax.dot_general(left, right, dims, preferred_element_type=F32)


def stacked(value):
    high, low = split(value)
    return jnp.concatenate([high, low], axis=0), high


def product(stack, high, s_high, s_low, dims):
    rows = high.shape[0]
    both = fast(stack, s_high, dims)
    return both[:rows] + both[rows:] + fast(high, s_low, dims)


def pack_gram(ref, gram):
    rank = gram.shape[0]
    ref[rank:, :] = jnp.zeros((SUBLANES, ref.shape[1]), F32)
    for group in range(rank // SUBLANES):
        rows = slice(group * SUBLANES, (group + 1) * SUBLANES)
        ref[rank:, group * rank : (group + 1) * rank] = gram[rows, :]


def unpack_gram(packed, rank):
    return jnp.concatenate(
        [packed[:, group * rank : (group + 1) * rank] for group in range(rank // SUBLANES)], axis=0
    )


def params(mib=32):
    return pltpu.CompilerParams(vmem_limit_bytes=mib << 20)


def vmem(count):
    return [pl.BlockSpec(memory_space=pltpu.VMEM)] * count


def cost(flops, moved):
    return pl.CostEstimate(flops=int(flops), bytes_accessed=int(moved), transcendentals=0)


def split_kernel(step, s_ref, copy_ref, high_ref, low_ref, sems):
    columns = s_ref.shape[1]
    copies = []
    for index in range(columns // step):
        here = pl.ds(index * step, step)
        copies.append(pltpu.make_async_copy(s_ref.at[:, here], copy_ref.at[:, here], sems.at[index]))
        copies[-1].start()
    for index, copy in enumerate(copies):
        here = pl.ds(index * step, step)
        copy.wait()
        high_ref[:, here], low_ref[:, here] = split(copy_ref[:, here])


def split_call(spectra):
    rows, columns = spectra.shape
    step = columns // 8 if columns % (8 * LANES) == 0 else columns
    return pl.pallas_call(
        functools.partial(split_kernel, step),
        in_specs=[pl.BlockSpec(memory_space=pltpu.HBM)],
        out_specs=vmem(3),
        out_shape=[
            jax.ShapeDtypeStruct((rows, columns), F32),
            jax.ShapeDtypeStruct((rows, columns), BF16),
            jax.ShapeDtypeStruct((rows, columns), BF16),
        ],
        scratch_shapes=[pltpu.SemaphoreType.DMA((columns // step,))],
        compiler_params=params(44),
        cost_estimate=cost(4 * rows * columns, 12 * rows * columns),
        name="split_spectra",
    )(spectra)


def bins_of(relative, width):
    block = jnp.bitwise_xor(lax.axis_index("px"), relative)
    return pl.ds(pl.multiple_of(block * width, LANES), width)


def scatter_kernel(relatives, width, w_ref, high_ref, low_ref, out):
    w = w_ref[...]
    rank = w.shape[0]
    stack, w_high = stacked(w)
    gram = product(stack, w_high, *split(w), NT)
    for index, relative in enumerate(relatives):
        here = bins_of(relative, width)
        out[index, :rank, :] = product(stack, w_high, high_ref[:, here], low_ref[:, here], NN)
        pack_gram(out.at[index], gram)


def scatter_call(relatives, width, w_block, high, low):
    rank, pixels = w_block.shape
    count = len(relatives)
    return pl.pallas_call(
        functools.partial(scatter_kernel, relatives, width),
        in_specs=vmem(3),
        out_specs=pl.BlockSpec(memory_space=pltpu.VMEM),
        out_shape=jax.ShapeDtypeStruct((count, rank + SUBLANES, width), F32),
        compiler_params=params(),
        cost_estimate=cost(6 * rank * pixels * width * count, 4 * pixels * width * count),
        name="loadings_times_spectra",
    )(w_block, high, low)


def pair_kernel(own_ref, other_ref, *outs):
    for index, out in enumerate(outs):
        out[...] = own_ref[index + 1] + other_ref[index + 1]


def pair_call(own, other):
    count = own.shape[0] - 1
    return pl.pallas_call(
        pair_kernel,
        in_specs=vmem(2),
        out_specs=vmem(count),
        out_shape=[jax.ShapeDtypeStruct(own.shape[1:], F32)] * count,
        compiler_params=params(),
        cost_estimate=cost(own.size, 12 * own.size),
        name="pair_sums",
    )(own, other)


def update_kernel(stacks, factor_ref, *refs):
    parts, out = refs[:-1], refs[-1]
    factor = factor_ref[...]
    rank = factor.shape[0]
    total = None
    for index, part in enumerate(parts):
        value = part[0] if index < stacks else part[...]
        total = value if total is None else total + value
    gram = unpack_gram(total[rank:], rank)
    out[...] = factor * total[:rank] / exact(gram, factor, NN)


def update_call(factor, stacks, parts):
    rank, width = factor.shape
    parts = (*stacks, *parts)
    return pl.pallas_call(
        functools.partial(update_kernel, len(stacks)),
        in_specs=vmem(1 + len(parts)),
        out_specs=pl.BlockSpec(memory_space=pltpu.VMEM),
        out_shape=jax.ShapeDtypeStruct((rank, width), F32),
        compiler_params=params(),
        cost_estimate=cost(12 * rank * rank * width, 4 * rank * width * (2 + len(parts))),
        name="update",
    )(factor, *parts)


def gather_kernel(relatives, carried, high_ref, low_ref, *refs):
    out = refs[-1]
    pieces = refs[: len(relatives)]
    rank, width = pieces[0].shape
    total, gram = None, None
    for relative, piece in zip(relatives, pieces):
        h = piece[...]
        stack, h_high = stacked(h)
        here = bins_of(relative, width)
        term = product(stack, h_high, high_ref[:, here], low_ref[:, here], NT)
        square = product(stack, h_high, *split(h), NT)
        total = term if total is None else total + term
        gram = square if gram is None else gram + square
    out[:rank, :] = total
    pack_gram(out, gram)
    if carried:
        out[...] += refs[len(relatives)][...]


def gather_call(relatives, pieces, high, low, before):
    rank, width = pieces[0].shape
    pixels = high.shape[0]
    extra = () if before is None else (before,)
    count = len(relatives)
    return pl.pallas_call(
        functools.partial(gather_kernel, relatives, before is not None),
        in_specs=vmem(2 + count + len(extra)),
        out_specs=pl.BlockSpec(memory_space=pltpu.VMEM),
        out_shape=jax.ShapeDtypeStruct((rank + SUBLANES, pixels), F32),
        compiler_params=params(),
        cost_estimate=cost(6 * rank * pixels * width * count, 4 * pixels * width * count),
        name="spectra_times_components",
    )(high, low, *pieces, *extra)


def thirds(value):
    high, low = split(value)
    return high, low, (value - high.astype(F32) - low.astype(F32)).astype(BF16)


def final_gather_kernel(relatives, groups, first, last, s_ref, w_ref, *refs):
    pieces, refs = refs[: len(relatives)], refs[len(relatives) :]
    carried, refs = ((), refs) if first else (refs[:3], refs[3:])
    rank, width = pieces[0].shape
    pixels = w_ref.shape[1]
    span = pixels // groups
    w = w_ref[...]
    w0, w1, w2 = thirds(w.T)
    left = jnp.concatenate([w0, w0, w1, w1, w2], axis=1)
    front = jnp.zeros((span, width), BF16)
    back = jnp.zeros((2 * LANES - span - rank, width), BF16)
    sums = [ref[...] for ref in carried] if carried else [None] * 3
    for relative, piece in zip(relatives, pieces):
        h0, h1 = split(piece[...])
        right = jnp.concatenate([h0, h1, h0, h1, h0], axis=0)
        d = s_ref[:, bins_of(relative, width)] - fast(left, right, NN)
        stack = jnp.concatenate([h0, h1], axis=0)
        error = product(stack, h0, *split(d), NT)
        gram = product(
            stack,
            h0,
            jnp.concatenate([front, h0, back], axis=0),
            jnp.concatenate([front, h1, back], axis=0),
            NT,
        )
        square = d * d
        folded = square[:, :LANES]
        for start in range(LANES, width, LANES):
            folded = folded + square[:, start : start + LANES]
        terms = (error, folded, gram)
        sums = [t if s is None else s + t for s, t in zip(sums, terms)]
    error, folded, gram = sums
    if not last:
        for ref, value in zip(refs, sums):
            ref[...] = value
        return
    outs, own_ref = refs[:groups], refs[groups]
    squares = exact(jnp.ones((SUBLANES, LANES), F32), folded, NT)
    table = jnp.concatenate([error, squares, w], axis=0)
    me = lax.axis_index("mz")
    free = LANES - span
    lane = lax.broadcasted_iota(jnp.int32, (rank, LANES), 1)
    for relative, out in enumerate(outs):
        group = jnp.bitwise_xor(me, relative)
        here = pltpu.roll(table, lax.rem(groups - group, groups) * span, 1)[:, :LANES]
        out[:rank, :] = jnp.where(lane < span, here[:rank], gram[:, :LANES])
        out[rank : rank + SUBLANES, :] = here[rank : rank + SUBLANES]
        out[rank + SUBLANES :, :] = jnp.zeros((SUBLANES, LANES), F32)
        rest = rank - free
        for index in range(rank // SUBLANES):
            rows = slice(index * SUBLANES, (index + 1) * SUBLANES)
            out[rank + SUBLANES :, index * rest : (index + 1) * rest] = gram[rows, LANES : LANES + rest]
        if relative == 0:
            own_ref[...] = here[rank + SUBLANES :, :span]


def final_gather_call(relatives, groups, pieces, spectra, w_block, before, last):
    rank, width = pieces[0].shape
    pixels = w_block.shape[1]
    count = len(relatives)
    first = before is None
    extra = () if first else tuple(before)
    shapes = [(rank, pixels), (pixels, LANES), (rank, 2 * LANES)]
    if last:
        shapes = [(rank + 2 * SUBLANES, LANES)] * groups + [(rank, pixels // groups)]
    return pl.pallas_call(
        functools.partial(final_gather_kernel, relatives, groups, first, last),
        in_specs=vmem(2 + count + len(extra)),
        out_specs=vmem(len(shapes)),
        out_shape=[jax.ShapeDtypeStruct(shape, F32) for shape in shapes],
        compiler_params=params(),
        cost_estimate=cost(18 * rank * pixels * width * count, 8 * pixels * width * count),
        name="final_products",
    )(spectra, w_block, *pieces, *extra)


def final_kernel(w_ref, h_ref, *refs):
    parts, (w_out, h_out, misfit_out) = refs[:-3], refs[-3:]
    h_out[...] = h_ref[...]
    w = w_ref[...]
    rank, span = w.shape
    total = parts[0][...]
    for part in parts[1:]:
        total = total + part[...]
    rest = rank - (LANES - span)
    low = total[rank + SUBLANES :]
    tail = [low[:, index * rest : (index + 1) * rest] for index in range(rank // SUBLANES)]
    gram = jnp.concatenate([total[:rank, span:], jnp.concatenate(tail, axis=0)], axis=1)
    error = total[:rank, :span]
    den = exact(gram, w, NN)
    new = w * (error + den) / den
    w_out[...] = new
    step = new - w
    change = step * (exact(gram, step, NN) - 2.0 * error)
    misfit_out[...] = total[rank : rank + 1, :span] + jnp.sum(change, axis=0, keepdims=True)


def final_call(w_piece, h_piece, *parts):
    rank, span = w_piece.shape
    return pl.pallas_call(
        final_kernel,
        in_specs=vmem(2 + len(parts)),
        out_specs=vmem(3),
        out_shape=[
            jax.ShapeDtypeStruct((rank, span), F32),
            jax.ShapeDtypeStruct(h_piece.shape, F32),
            jax.ShapeDtypeStruct((1, span), F32),
        ],
        compiler_params=params(),
        cost_estimate=cost(24 * rank * rank * span, 4 * rank * LANES * len(parts)),
        name="final_update",
    )(w_piece, h_piece, *parts)


def join_kernel(*refs):
    pieces, out = refs[:-1], refs[-1]
    _, width = pieces[0].shape
    whole = jnp.concatenate([piece[...] for piece in pieces], axis=1)
    out[...] = pltpu.roll(whole, lax.axis_index("mz") * width, 1)


def join_call(*pieces):
    rank, width = pieces[0].shape
    return pl.pallas_call(
        join_kernel,
        in_specs=vmem(len(pieces)),
        out_specs=pl.BlockSpec(memory_space=pltpu.VMEM),
        out_shape=jax.ShapeDtypeStruct((rank, width * len(pieces)), F32),
        compiler_params=params(),
        cost_estimate=cost(0, 8 * rank * width * len(pieces)),
        name="join",
    )(*pieces)


def swap(value, axis, size, mask):
    return lax.ppermute(value, axis, [(i, i ^ mask) for i in range(size)])


def cross(value, groups, owners, even, odd):
    pairs = [
        (g * owners + o, (g ^ (even if o % 2 else odd)) * owners + o)
        for g in range(groups)
        for o in range(owners)
    ]
    return lax.ppermute(value, ("mz", "px"), pairs)


def spread(h_piece, owners, products):
    evens = [owners - 2, *range(2, owners - 2, 2)]
    mine = []
    for relative in evens:
        mine.append(swap(h_piece, "px", owners, relative))
    beside = swap(h_piece, "px", owners, 1)
    theirs = []
    for piece in mine:
        theirs.append(swap(piece, "px", owners, 1))
    total = products([0, 1], [h_piece, beside], None, False)
    total = products(evens, mine, total, False)
    return products([r + 1 for r in evens], theirs, total, True)


def fast_device(groups, owners, spectra, w_piece, h_piece):
    width = h_piece.shape[1]
    copy, high, low = split_call(spectra)
    w_block = join_call(
        w_piece,
        *[
            lax.ppermute(w_piece, "mz", [(i, (i - k) % groups) for i in range(groups)])
            for k in range(1, groups)
        ],
    )
    evens = list(range(owners - 2, 0, -2))
    steps = [(1, 1)]
    if groups > 2:
        steps = [*[(k, k) for k in range(groups - 1, 2, -1)], (1, 2), (2, 1)]
    for iteration in range(ITERS):
        theirs = scatter_call(list(range(1, owners, 2)), width, w_block, high, low)
        other = swap(theirs, "px", owners, 1)
        own = scatter_call(list(range(0, owners, 2)), width, w_block, high, low)
        sums = pair_call(own, other)
        sent = [swap(sums[r // 2 - 1], "px", owners, r) for r in evens]
        h_piece = update_call(h_piece, (own, other), sent)
        if iteration + 1 < ITERS:
            total = spread(
                h_piece,
                owners,
                lambda relatives, pieces, before, last: gather_call(relatives, pieces, high, low, before),
            )
            sent = []
            for even, odd in steps:
                sent.append(cross(total, groups, owners, even, odd))
            w_block = update_call(w_block, (), (total, *sent))
        else:
            parts = spread(
                h_piece,
                owners,
                lambda relatives, pieces, before, last: final_gather_call(
                    relatives, groups, pieces, copy, w_block, before, last
                ),
            )
            sent = []
            for k in [*range(2, groups), 1]:
                sent.append(swap(parts[k], "mz", groups, k))
            w_final, h_final, misfit = final_call(parts[groups], h_piece, parts[0], *sent)
    return w_final, h_final, misfit.reshape(-1)


def per_device(groups, owners, spectra, w_piece, h_piece):
    rank = w_piece.shape[0]
    pixels, width = spectra.shape[0], h_piece.shape[1]

    def power(n):
        return n > 1 and n & (n - 1) == 0

    fits = (
        power(groups)
        and power(owners)
        and width % LANES == 0
        and pixels % LANES == 0
        and w_piece.shape[1] % SUBLANES == 0
        and rank % (2 * SUBLANES) == 0
        and rank // SUBLANES * rank <= min(width, pixels)
        and w_piece.shape[1] < LANES
        and LANES - w_piece.shape[1] < rank
        and (rank - LANES + w_piece.shape[1]) * (rank // SUBLANES) <= LANES
    )
    if fits:
        return fast_device(groups, owners, spectra, w_piece, h_piece)
    return plain_device(spectra, w_piece, h_piece)


def solution(mesh):
    in_specs = (P("px", "mz"), P(None, ("px", "mz")), P(None, ("mz", "px")))
    out_specs = (P(None, ("px", "mz")), P(None, ("mz", "px")), P(("px", "mz")))
    body = functools.partial(per_device, mesh.shape["mz"], mesh.shape["px"])
    return jax.shard_map(body, mesh=mesh, in_specs=in_specs, out_specs=out_specs, check_vma=False)
```

```python
import functools

import jax
import jax.numpy as jnp
from jax import lax
from jax.experimental import pallas as pl
from jax.experimental.pallas import tpu as pltpu
from jax.sharding import PartitionSpec as P


ITERS = 3
LANES = 128
SUBLANES = 8
F32 = jnp.float32
BF16 = jnp.bfloat16
NN = (((1,), (0,)), ((), ()))
NT = (((1,), (1,)), ((), ()))


def matmul(left, right):
    return jnp.dot(left, right, preferred_element_type=F32, precision=lax.Precision.HIGHEST)


def plain_device(spectra, w_piece, h_piece):
    def rows_of(piece):
        return lax.all_gather(piece, "mz", axis=1, tiled=True)

    w_block = rows_of(w_piece)
    for _ in range(ITERS):
        numerator = lax.psum_scatter(matmul(w_block, spectra), "px", scatter_dimension=1, tiled=True)
        gram_w = lax.psum(matmul(w_block, w_block.T), "px")
        h_piece = h_piece * numerator / matmul(gram_w, h_piece)
        h_block = lax.all_gather(h_piece, "px", axis=1, tiled=True)
        numerator = lax.psum_scatter(matmul(h_block, spectra.T), "mz", scatter_dimension=1, tiled=True)
        gram_h = lax.psum(matmul(h_block, h_block.T), "mz")
        w_piece = w_piece * numerator / matmul(gram_h, w_piece)
        w_block = rows_of(w_piece)
    difference = spectra - matmul(w_block.T, h_block)
    partial_error = jnp.sum(difference * difference, axis=1)
    misfit = lax.psum_scatter(partial_error, "mz", scatter_dimension=0, tiled=True)
    return (w_piece, h_piece, misfit)


def split(value):
    high = value.astype(BF16)
    return high, (value - high.astype(F32)).astype(BF16)


def exact(left, right, dims):
    return lax.dot_general(left, right, dims, precision=lax.Precision.HIGHEST, preferred_element_type=F32)


def fast(left, right, dims):
    return lax.dot_general(left, right, dims, preferred_element_type=F32)


def stacked(value):
    high, low = split(value)
    return jnp.concatenate([high, low], axis=0), high


def product(stack, high, s_high, s_low, dims):
    rows = high.shape[0]
    both = fast(stack, s_high, dims)
    return both[:rows] + both[rows:] + fast(high, s_low, dims)


def pack_gram(ref, gram):
    rank = gram.shape[0]
    ref[rank:, :] = jnp.zeros((SUBLANES, ref.shape[1]), F32)
    for group in range(rank // SUBLANES):
        rows = slice(group * SUBLANES, (group + 1) * SUBLANES)
        ref[rank:, group * rank : (group + 1) * rank] = gram[rows, :]


def unpack_gram(packed, rank):
    return jnp.concatenate(
        [packed[:, group * rank : (group + 1) * rank] for group in range(rank // SUBLANES)], axis=0
    )


def params(mib=32):
    return pltpu.CompilerParams(vmem_limit_bytes=mib << 20)


def vmem(count):
    return [pl.BlockSpec(memory_space=pltpu.VMEM)] * count


def cost(flops, moved):
    return pl.CostEstimate(flops=int(flops), bytes_accessed=int(moved), transcendentals=0)


def split_kernel(step, s_ref, copy_ref, high_ref, low_ref, sems):
    columns = s_ref.shape[1]
    copies = []
    for index in range(columns // step):
        here = pl.ds(index * step, step)
        copies.append(pltpu.make_async_copy(s_ref.at[:, here], copy_ref.at[:, here], sems.at[index]))
        copies[-1].start()
    for index, copy in enumerate(copies):
        here = pl.ds(index * step, step)
        copy.wait()
        high_ref[:, here], low_ref[:, here] = split(copy_ref[:, here])


def split_call(spectra):
    rows, columns = spectra.shape
    step = columns // 8 if columns % (8 * LANES) == 0 else columns
    return pl.pallas_call(
        functools.partial(split_kernel, step),
        in_specs=[pl.BlockSpec(memory_space=pltpu.HBM)],
        out_specs=vmem(3),
        out_shape=[
            jax.ShapeDtypeStruct((rows, columns), F32),
            jax.ShapeDtypeStruct((rows, columns), BF16),
            jax.ShapeDtypeStruct((rows, columns), BF16),
        ],
        scratch_shapes=[pltpu.SemaphoreType.DMA((columns // step,))],
        compiler_params=params(44),
        cost_estimate=cost(4 * rows * columns, 12 * rows * columns),
        name="split_spectra",
    )(spectra)


def bins_of(relative, width):
    block = jnp.bitwise_xor(lax.axis_index("px"), relative)
    return pl.ds(pl.multiple_of(block * width, LANES), width)


def scatter_kernel(relatives, width, w_ref, high_ref, low_ref, *outs):
    if len(outs[0].shape) == 3:
        outs = [outs[0].at[index] for index in range(len(relatives))]
    w = w_ref[...]
    rank = w.shape[0]
    stack, w_high = stacked(w)
    gram = product(stack, w_high, *split(w), NT)
    for relative, out in zip(relatives, outs):
        here = bins_of(relative, width)
        out[:rank, :] = product(stack, w_high, high_ref[:, here], low_ref[:, here], NN)
        pack_gram(out, gram)


def scatter_call(relatives, width, w_block, high, low, joined=True):
    rank, pixels = w_block.shape
    count = len(relatives)
    shape = (rank + SUBLANES, width)
    shapes = [(count, *shape)] if joined else [shape] * count
    return pl.pallas_call(
        functools.partial(scatter_kernel, relatives, width),
        in_specs=vmem(3),
        out_specs=vmem(len(shapes)),
        out_shape=[jax.ShapeDtypeStruct(shape, F32) for shape in shapes],
        compiler_params=params(),
        cost_estimate=cost(6 * rank * pixels * width * count, 4 * pixels * width * count),
        name="loadings_times_spectra",
    )(w_block, high, low)


def pair_kernel(own_ref, other_ref, *outs):
    for index, out in enumerate(outs):
        out[...] = own_ref[index] + other_ref[index]


def pair_call(own, other):
    count = own.shape[0]
    return pl.pallas_call(
        pair_kernel,
        in_specs=vmem(2),
        out_specs=vmem(count),
        out_shape=[jax.ShapeDtypeStruct(own.shape[1:], F32)] * count,
        compiler_params=params(),
        cost_estimate=cost(own.size, 12 * own.size),
        name="pair_sums",
    )(own, other)


def update_kernel(factor_ref, *refs):
    parts, out = refs[:-1], refs[-1]
    factor = factor_ref[...]
    rank = factor.shape[0]
    total = parts[0][...]
    for part in parts[1:]:
        total = total + part[...]
    gram = unpack_gram(total[rank:], rank)
    out[...] = factor * total[:rank] / exact(gram, factor, NN)


def update_call(factor, *parts):
    rank, width = factor.shape
    return pl.pallas_call(
        update_kernel,
        in_specs=vmem(1 + len(parts)),
        out_specs=pl.BlockSpec(memory_space=pltpu.VMEM),
        out_shape=jax.ShapeDtypeStruct((rank, width), F32),
        compiler_params=params(),
        cost_estimate=cost(12 * rank * rank * width, 4 * rank * width * (2 + len(parts))),
        name="update",
    )(factor, *parts)


def gather_kernel(relatives, carried, high_ref, low_ref, *refs):
    out = refs[-1]
    pieces = refs[: len(relatives)]
    rank, width = pieces[0].shape
    total, gram = None, None
    for relative, piece in zip(relatives, pieces):
        h = piece[...]
        stack, h_high = stacked(h)
        here = bins_of(relative, width)
        term = product(stack, h_high, high_ref[:, here], low_ref[:, here], NT)
        square = product(stack, h_high, *split(h), NT)
        total = term if total is None else total + term
        gram = square if gram is None else gram + square
    out[:rank, :] = total
    pack_gram(out, gram)
    if carried:
        out[...] += refs[len(relatives)][...]


def gather_call(relatives, pieces, high, low, before):
    rank, width = pieces[0].shape
    pixels = high.shape[0]
    extra = () if before is None else (before,)
    count = len(relatives)
    return pl.pallas_call(
        functools.partial(gather_kernel, relatives, before is not None),
        in_specs=vmem(2 + count + len(extra)),
        out_specs=pl.BlockSpec(memory_space=pltpu.VMEM),
        out_shape=jax.ShapeDtypeStruct((rank + SUBLANES, pixels), F32),
        compiler_params=params(),
        cost_estimate=cost(6 * rank * pixels * width * count, 4 * pixels * width * count),
        name="spectra_times_components",
    )(high, low, *pieces, *extra)


def thirds(value):
    high, low = split(value)
    return high, low, (value - high.astype(F32) - low.astype(F32)).astype(BF16)


def final_gather_kernel(relatives, groups, first, last, s_ref, w_ref, *refs):
    pieces, refs = refs[: len(relatives)], refs[len(relatives) :]
    carried, refs = ((), refs) if first else (refs[:3], refs[3:])
    rank, width = pieces[0].shape
    pixels = w_ref.shape[1]
    span = pixels // groups
    w = w_ref[...]
    w0, w1, w2 = thirds(w.T)
    left = jnp.concatenate([w0, w0, w1, w1, w2], axis=1)
    front = jnp.zeros((span, width), BF16)
    back = jnp.zeros((2 * LANES - span - rank, width), BF16)
    sums = [ref[...] for ref in carried] if carried else [None] * 3
    for relative, piece in zip(relatives, pieces):
        h0, h1 = split(piece[...])
        right = jnp.concatenate([h0, h1, h0, h1, h0], axis=0)
        d = s_ref[:, bins_of(relative, width)] - fast(left, right, NN)
        stack = jnp.concatenate([h0, h1], axis=0)
        error = product(stack, h0, *split(d), NT)
        gram = product(
            stack,
            h0,
            jnp.concatenate([front, h0, back], axis=0),
            jnp.concatenate([front, h1, back], axis=0),
            NT,
        )
        square = d * d
        folded = square[:, :LANES]
        for start in range(LANES, width, LANES):
            folded = folded + square[:, start : start + LANES]
        terms = (error, folded, gram)
        sums = [t if s is None else s + t for s, t in zip(sums, terms)]
    error, folded, gram = sums
    if not last:
        for ref, value in zip(refs, sums):
            ref[...] = value
        return
    outs, own_ref = refs[:groups], refs[groups]
    squares = exact(jnp.ones((SUBLANES, LANES), F32), folded, NT)
    table = jnp.concatenate([error, squares, w], axis=0)
    me = lax.axis_index("mz")
    free = LANES - span
    lane = lax.broadcasted_iota(jnp.int32, (rank, LANES), 1)
    for relative, out in enumerate(outs):
        group = jnp.bitwise_xor(me, relative)
        here = pltpu.roll(table, lax.rem(groups - group, groups) * span, 1)[:, :LANES]
        out[:rank, :] = jnp.where(lane < span, here[:rank], gram[:, :LANES])
        out[rank : rank + SUBLANES, :] = here[rank : rank + SUBLANES]
        out[rank + SUBLANES :, :] = jnp.zeros((SUBLANES, LANES), F32)
        rest = rank - free
        for index in range(rank // SUBLANES):
            rows = slice(index * SUBLANES, (index + 1) * SUBLANES)
            out[rank + SUBLANES :, index * rest : (index + 1) * rest] = gram[rows, LANES : LANES + rest]
        if relative == 0:
            own_ref[...] = here[rank + SUBLANES :, :span]


def final_gather_call(relatives, groups, pieces, spectra, w_block, before, last):
    rank, width = pieces[0].shape
    pixels = w_block.shape[1]
    count = len(relatives)
    first = before is None
    extra = () if first else tuple(before)
    shapes = [(rank, pixels), (pixels, LANES), (rank, 2 * LANES)]
    if last:
        shapes = [(rank + 2 * SUBLANES, LANES)] * groups + [(rank, pixels // groups)]
    return pl.pallas_call(
        functools.partial(final_gather_kernel, relatives, groups, first, last),
        in_specs=vmem(2 + count + len(extra)),
        out_specs=vmem(len(shapes)),
        out_shape=[jax.ShapeDtypeStruct(shape, F32) for shape in shapes],
        compiler_params=params(),
        cost_estimate=cost(18 * rank * pixels * width * count, 8 * pixels * width * count),
        name="final_products",
    )(spectra, w_block, *pieces, *extra)


def final_kernel(w_ref, h_ref, *refs):
    parts, (w_out, h_out, misfit_out) = refs[:-3], refs[-3:]
    h_out[...] = h_ref[...]
    w = w_ref[...]
    rank, span = w.shape
    total = parts[0][...]
    for part in parts[1:]:
        total = total + part[...]
    rest = rank - (LANES - span)
    low = total[rank + SUBLANES :]
    tail = [low[:, index * rest : (index + 1) * rest] for index in range(rank // SUBLANES)]
    gram = jnp.concatenate([total[:rank, span:], jnp.concatenate(tail, axis=0)], axis=1)
    error = total[:rank, :span]
    den = exact(gram, w, NN)
    new = w * (error + den) / den
    w_out[...] = new
    step = new - w
    change = step * (exact(gram, step, NN) - 2.0 * error)
    misfit_out[...] = total[rank : rank + 1, :span] + jnp.sum(change, axis=0, keepdims=True)


def final_call(w_piece, h_piece, *parts):
    rank, span = w_piece.shape
    return pl.pallas_call(
        final_kernel,
        in_specs=vmem(2 + len(parts)),
        out_specs=vmem(3),
        out_shape=[
            jax.ShapeDtypeStruct((rank, span), F32),
            jax.ShapeDtypeStruct(h_piece.shape, F32),
            jax.ShapeDtypeStruct((1, span), F32),
        ],
        compiler_params=params(),
        cost_estimate=cost(24 * rank * rank * span, 4 * rank * LANES * len(parts)),
        name="final_update",
    )(w_piece, h_piece, *parts)


def join_kernel(*refs):
    pieces, out = refs[:-1], refs[-1]
    _, width = pieces[0].shape
    whole = jnp.concatenate([piece[...] for piece in pieces], axis=1)
    out[...] = pltpu.roll(whole, lax.axis_index("mz") * width, 1)


def join_call(*pieces):
    rank, width = pieces[0].shape
    return pl.pallas_call(
        join_kernel,
        in_specs=vmem(len(pieces)),
        out_specs=pl.BlockSpec(memory_space=pltpu.VMEM),
        out_shape=jax.ShapeDtypeStruct((rank, width * len(pieces)), F32),
        compiler_params=params(),
        cost_estimate=cost(0, 8 * rank * width * len(pieces)),
        name="join",
    )(*pieces)


def swap(value, axis, size, mask):
    return lax.ppermute(value, axis, [(i, i ^ mask) for i in range(size)])


def cross(value, groups, owners, even, odd):
    pairs = [
        (g * owners + o, (g ^ (even if o % 2 else odd)) * owners + o)
        for g in range(groups)
        for o in range(owners)
    ]
    return lax.ppermute(value, ("mz", "px"), pairs)


def spread(h_piece, owners, products):
    evens = [owners - 2, *range(2, owners - 2, 2)]
    mine = []
    for relative in evens:
        mine.append(swap(h_piece, "px", owners, relative))
    beside = swap(h_piece, "px", owners, 1)
    theirs = []
    for piece in mine:
        theirs.append(swap(piece, "px", owners, 1))
    total = products([0, 1], [h_piece, beside], None, False)
    total = products(evens, mine, total, False)
    return products([r + 1 for r in evens], theirs, total, True)


def fast_device(groups, owners, spectra, w_piece, h_piece):
    width = h_piece.shape[1]
    copy, high, low = split_call(spectra)
    w_block = join_call(
        w_piece,
        *[
            lax.ppermute(w_piece, "mz", [(i, (i - k) % groups) for i in range(groups)])
            for k in range(1, groups)
        ],
    )
    evens = list(range(owners - 2, 0, -2))
    steps = [(1, 1)]
    if groups > 2:
        steps = [*[(k, k) for k in range(groups - 1, 2, -1)], (1, 2), (2, 1)]
    for iteration in range(ITERS):
        batches = [evens[:1], evens[1:]] if len(evens) > 1 else [evens]
        others = []
        for batch in batches:
            (theirs,) = scatter_call([r + 1 for r in batch], width, w_block, high, low)
            others.append(swap(theirs, "px", owners, 1))
        sent = []
        for batch, other in zip(batches, others):
            (own,) = scatter_call(batch, width, w_block, high, low)
            for relative, value in zip(batch, pair_call(own, other)):
                sent.append(swap(value, "px", owners, relative))
        beside, near = scatter_call([1, 0], width, w_block, high, low, False)
        beside = swap(beside, "px", owners, 1)
        h_piece = update_call(h_piece, near, beside, *sent)
        if iteration + 1 < ITERS:
            total = spread(
                h_piece,
                owners,
                lambda relatives, pieces, before, last: gather_call(relatives, pieces, high, low, before),
            )
            sent = []
            for even, odd in steps:
                sent.append(cross(total, groups, owners, even, odd))
            w_block = update_call(w_block, total, *sent)
        else:
            parts = spread(
                h_piece,
                owners,
                lambda relatives, pieces, before, last: final_gather_call(
                    relatives, groups, pieces, copy, w_block, before, last
                ),
            )
            sent = []
            for k in [*range(2, groups), 1]:
                sent.append(swap(parts[k], "mz", groups, k))
            w_final, h_final, misfit = final_call(parts[groups], h_piece, parts[0], *sent)
    return w_final, h_final, misfit.reshape(-1)


def per_device(groups, owners, spectra, w_piece, h_piece):
    rank = w_piece.shape[0]
    pixels, width = spectra.shape[0], h_piece.shape[1]

    def power(n):
        return n > 1 and n & (n - 1) == 0

    fits = (
        power(groups)
        and power(owners)
        and width % LANES == 0
        and pixels % LANES == 0
        and w_piece.shape[1] % SUBLANES == 0
        and rank % (2 * SUBLANES) == 0
        and rank // SUBLANES * rank <= min(width, pixels)
        and w_piece.shape[1] < LANES
        and LANES - w_piece.shape[1] < rank
        and (rank - LANES + w_piece.shape[1]) * (rank // SUBLANES) <= LANES
    )
    if fits:
        return fast_device(groups, owners, spectra, w_piece, h_piece)
    return plain_device(spectra, w_piece, h_piece)


def solution(mesh):
    in_specs = (P("px", "mz"), P(None, ("px", "mz")), P(None, ("mz", "px")))
    out_specs = (P(None, ("px", "mz")), P(None, ("mz", "px")), P(("px", "mz")))
    body = functools.partial(per_device, mesh.shape["mz"], mesh.shape["px"])
    return jax.shard_map(body, mesh=mesh, in_specs=in_specs, out_specs=out_specs, check_vma=False)
```

```python
import functools

import jax
import jax.numpy as jnp
from jax import lax
from jax.experimental import pallas as pl
from jax.experimental.pallas import tpu as pltpu
from jax.sharding import PartitionSpec as P


ITERS = 3
LANES = 128
SUBLANES = 8
F32 = jnp.float32
BF16 = jnp.bfloat16
NN = (((1,), (0,)), ((), ()))
NT = (((1,), (1,)), ((), ()))


def matmul(left, right):
    return jnp.dot(left, right, preferred_element_type=F32, precision=lax.Precision.HIGHEST)


def plain_device(spectra, w_piece, h_piece):
    def rows_of(piece):
        return lax.all_gather(piece, "mz", axis=1, tiled=True)

    w_block = rows_of(w_piece)
    for _ in range(ITERS):
        numerator = lax.psum_scatter(matmul(w_block, spectra), "px", scatter_dimension=1, tiled=True)
        gram_w = lax.psum(matmul(w_block, w_block.T), "px")
        h_piece = h_piece * numerator / matmul(gram_w, h_piece)
        h_block = lax.all_gather(h_piece, "px", axis=1, tiled=True)
        numerator = lax.psum_scatter(matmul(h_block, spectra.T), "mz", scatter_dimension=1, tiled=True)
        gram_h = lax.psum(matmul(h_block, h_block.T), "mz")
        w_piece = w_piece * numerator / matmul(gram_h, w_piece)
        w_block = rows_of(w_piece)
    difference = spectra - matmul(w_block.T, h_block)
    partial_error = jnp.sum(difference * difference, axis=1)
    misfit = lax.psum_scatter(partial_error, "mz", scatter_dimension=0, tiled=True)
    return (w_piece, h_piece, misfit)


def split(value):
    high = value.astype(BF16)
    return high, (value - high.astype(F32)).astype(BF16)


def exact(left, right, dims):
    return lax.dot_general(left, right, dims, precision=lax.Precision.HIGHEST, preferred_element_type=F32)


def fast(left, right, dims):
    return lax.dot_general(left, right, dims, preferred_element_type=F32)


def stacked(value):
    high, low = split(value)
    return jnp.concatenate([high, low], axis=0), high


def product(stack, high, s_high, s_low, dims):
    rows = high.shape[0]
    both = fast(stack, s_high, dims)
    return both[:rows] + both[rows:] + fast(high, s_low, dims)


def pack_gram(ref, gram):
    rank = gram.shape[0]
    ref[rank:, :] = jnp.zeros((SUBLANES, ref.shape[1]), F32)
    for group in range(rank // SUBLANES):
        rows = slice(group * SUBLANES, (group + 1) * SUBLANES)
        ref[rank:, group * rank : (group + 1) * rank] = gram[rows, :]


def unpack_gram(packed, rank):
    return jnp.concatenate(
        [packed[:, group * rank : (group + 1) * rank] for group in range(rank // SUBLANES)], axis=0
    )


def params(mib=32):
    return pltpu.CompilerParams(vmem_limit_bytes=mib << 20)


def vmem(count):
    return [pl.BlockSpec(memory_space=pltpu.VMEM)] * count


def cost(flops, moved):
    return pl.CostEstimate(flops=int(flops), bytes_accessed=int(moved), transcendentals=0)


def split_kernel(step, s_ref, copy_ref, high_ref, low_ref, sems):
    columns = s_ref.shape[1]
    copies = []
    for index in range(columns // step):
        here = pl.ds(index * step, step)
        copies.append(pltpu.make_async_copy(s_ref.at[:, here], copy_ref.at[:, here], sems.at[index]))
        copies[-1].start()
    for index, copy in enumerate(copies):
        here = pl.ds(index * step, step)
        copy.wait()
        high_ref[:, here], low_ref[:, here] = split(copy_ref[:, here])


def split_call(spectra):
    rows, columns = spectra.shape
    step = columns // 8 if columns % (8 * LANES) == 0 else columns
    return pl.pallas_call(
        functools.partial(split_kernel, step),
        in_specs=[pl.BlockSpec(memory_space=pltpu.HBM)],
        out_specs=vmem(3),
        out_shape=[
            jax.ShapeDtypeStruct((rows, columns), F32),
            jax.ShapeDtypeStruct((rows, columns), BF16),
            jax.ShapeDtypeStruct((rows, columns), BF16),
        ],
        scratch_shapes=[pltpu.SemaphoreType.DMA((columns // step,))],
        compiler_params=params(44),
        cost_estimate=cost(4 * rows * columns, 12 * rows * columns),
        name="split_spectra",
    )(spectra)


def bins_of(relative, width):
    block = jnp.bitwise_xor(lax.axis_index("px"), relative)
    return pl.ds(pl.multiple_of(block * width, LANES), width)


def scatter_kernel(relatives, width, w_ref, high_ref, low_ref, *outs):
    if len(outs[0].shape) == 3:
        outs = [outs[0].at[index] for index in range(len(relatives))]
    w = w_ref[...]
    rank = w.shape[0]
    stack, w_high = stacked(w)
    gram = product(stack, w_high, *split(w), NT)
    for relative, out in zip(relatives, outs):
        here = bins_of(relative, width)
        out[:rank, :] = product(stack, w_high, high_ref[:, here], low_ref[:, here], NN)
        pack_gram(out, gram)


def scatter_call(relatives, width, w_block, high, low, joined=True):
    rank, pixels = w_block.shape
    count = len(relatives)
    shape = (rank + SUBLANES, width)
    shapes = [(count, *shape)] if joined else [shape] * count
    return pl.pallas_call(
        functools.partial(scatter_kernel, relatives, width),
        in_specs=vmem(3),
        out_specs=vmem(len(shapes)),
        out_shape=[jax.ShapeDtypeStruct(shape, F32) for shape in shapes],
        compiler_params=params(),
        cost_estimate=cost(6 * rank * pixels * width * count, 4 * pixels * width * count),
        name="loadings_times_spectra",
    )(w_block, high, low)


def pair_kernel(own_ref, other_ref, *outs):
    for index, out in enumerate(outs):
        out[...] = own_ref[index] + other_ref[index]


def pair_call(own, other):
    count = own.shape[0]
    return pl.pallas_call(
        pair_kernel,
        in_specs=vmem(2),
        out_specs=vmem(count),
        out_shape=[jax.ShapeDtypeStruct(own.shape[1:], F32)] * count,
        compiler_params=params(),
        cost_estimate=cost(own.size, 12 * own.size),
        name="pair_sums",
    )(own, other)


def update_kernel(factor_ref, *refs):
    parts, out = refs[:-1], refs[-1]
    factor = factor_ref[...]
    rank = factor.shape[0]
    total = parts[0][...]
    for part in parts[1:]:
        total = total + part[...]
    gram = unpack_gram(total[rank:], rank)
    out[...] = factor * total[:rank] / exact(gram, factor, NN)


def update_call(factor, *parts):
    rank, width = factor.shape
    return pl.pallas_call(
        update_kernel,
        in_specs=vmem(1 + len(parts)),
        out_specs=pl.BlockSpec(memory_space=pltpu.VMEM),
        out_shape=jax.ShapeDtypeStruct((rank, width), F32),
        compiler_params=params(),
        cost_estimate=cost(12 * rank * rank * width, 4 * rank * width * (2 + len(parts))),
        name="update",
    )(factor, *parts)


def gather_kernel(relatives, carried, high_ref, low_ref, *refs):
    out = refs[-1]
    pieces = refs[: len(relatives)]
    rank, width = pieces[0].shape
    total, gram = None, None
    for relative, piece in zip(relatives, pieces):
        h = piece[...]
        stack, h_high = stacked(h)
        here = bins_of(relative, width)
        term = product(stack, h_high, high_ref[:, here], low_ref[:, here], NT)
        square = product(stack, h_high, *split(h), NT)
        total = term if total is None else total + term
        gram = square if gram is None else gram + square
    out[:rank, :] = total
    pack_gram(out, gram)
    if carried:
        out[...] += refs[len(relatives)][...]


def gather_call(relatives, pieces, high, low, before):
    rank, width = pieces[0].shape
    pixels = high.shape[0]
    extra = () if before is None else (before,)
    count = len(relatives)
    return pl.pallas_call(
        functools.partial(gather_kernel, relatives, before is not None),
        in_specs=vmem(2 + count + len(extra)),
        out_specs=pl.BlockSpec(memory_space=pltpu.VMEM),
        out_shape=jax.ShapeDtypeStruct((rank + SUBLANES, pixels), F32),
        compiler_params=params(),
        cost_estimate=cost(6 * rank * pixels * width * count, 4 * pixels * width * count),
        name="spectra_times_components",
    )(high, low, *pieces, *extra)


def thirds(value):
    high, low = split(value)
    return high, low, (value - high.astype(F32) - low.astype(F32)).astype(BF16)


def final_gather_kernel(relatives, groups, first, last, s_ref, w_ref, *refs):
    pieces, refs = refs[: len(relatives)], refs[len(relatives) :]
    carried, refs = ((), refs) if first else (refs[:3], refs[3:])
    rank, width = pieces[0].shape
    pixels = w_ref.shape[1]
    span = pixels // groups
    w = w_ref[...]
    w0, w1, w2 = thirds(w.T)
    left = jnp.concatenate([w0, w0, w1, w1, w2], axis=1)
    front = jnp.zeros((span, width), BF16)
    back = jnp.zeros((2 * LANES - span - rank, width), BF16)
    sums = [ref[...] for ref in carried] if carried else [None] * 3
    for relative, piece in zip(relatives, pieces):
        h0, h1 = split(piece[...])
        right = jnp.concatenate([h0, h1, h0, h1, h0], axis=0)
        d = s_ref[:, bins_of(relative, width)] - fast(left, right, NN)
        stack = jnp.concatenate([h0, h1], axis=0)
        error = product(stack, h0, *split(d), NT)
        gram = product(
            stack,
            h0,
            jnp.concatenate([front, h0, back], axis=0),
            jnp.concatenate([front, h1, back], axis=0),
            NT,
        )
        square = d * d
        folded = square[:, :LANES]
        for start in range(LANES, width, LANES):
            folded = folded + square[:, start : start + LANES]
        terms = (error, folded, gram)
        sums = [t if s is None else s + t for s, t in zip(sums, terms)]
    error, folded, gram = sums
    if not last:
        for ref, value in zip(refs, sums):
            ref[...] = value
        return
    outs, own_ref = refs[:groups], refs[groups]
    squares = exact(jnp.ones((SUBLANES, LANES), F32), folded, NT)
    table = jnp.concatenate([error, squares, w], axis=0)
    me = lax.axis_index("mz")
    free = LANES - span
    lane = lax.broadcasted_iota(jnp.int32, (rank, LANES), 1)
    for relative, out in enumerate(outs):
        group = jnp.bitwise_xor(me, relative)
        here = pltpu.roll(table, lax.rem(groups - group, groups) * span, 1)[:, :LANES]
        out[:rank, :] = jnp.where(lane < span, here[:rank], gram[:, :LANES])
        out[rank : rank + SUBLANES, :] = here[rank : rank + SUBLANES]
        out[rank + SUBLANES :, :] = jnp.zeros((SUBLANES, LANES), F32)
        rest = rank - free
        for index in range(rank // SUBLANES):
            rows = slice(index * SUBLANES, (index + 1) * SUBLANES)
            out[rank + SUBLANES :, index * rest : (index + 1) * rest] = gram[rows, LANES : LANES + rest]
        if relative == 0:
            own_ref[...] = here[rank + SUBLANES :, :span]


def final_gather_call(relatives, groups, pieces, spectra, w_block, before, last):
    rank, width = pieces[0].shape
    pixels = w_block.shape[1]
    count = len(relatives)
    first = before is None
    extra = () if first else tuple(before)
    shapes = [(rank, pixels), (pixels, LANES), (rank, 2 * LANES)]
    if last:
        shapes = [(rank + 2 * SUBLANES, LANES)] * groups + [(rank, pixels // groups)]
    return pl.pallas_call(
        functools.partial(final_gather_kernel, relatives, groups, first, last),
        in_specs=vmem(2 + count + len(extra)),
        out_specs=vmem(len(shapes)),
        out_shape=[jax.ShapeDtypeStruct(shape, F32) for shape in shapes],
        compiler_params=params(),
        cost_estimate=cost(18 * rank * pixels * width * count, 8 * pixels * width * count),
        name="final_products",
    )(spectra, w_block, *pieces, *extra)


def final_kernel(w_ref, h_ref, *refs):
    parts, (w_out, h_out, misfit_out) = refs[:-3], refs[-3:]
    h_out[...] = h_ref[...]
    w = w_ref[...]
    rank, span = w.shape
    total = parts[0][...]
    for part in parts[1:]:
        total = total + part[...]
    rest = rank - (LANES - span)
    low = total[rank + SUBLANES :]
    tail = [low[:, index * rest : (index + 1) * rest] for index in range(rank // SUBLANES)]
    gram = jnp.concatenate([total[:rank, span:], jnp.concatenate(tail, axis=0)], axis=1)
    error = total[:rank, :span]
    den = exact(gram, w, NN)
    new = w * (error + den) / den
    w_out[...] = new
    step = new - w
    change = step * (exact(gram, step, NN) - 2.0 * error)
    misfit_out[...] = total[rank : rank + 1, :span] + jnp.sum(change, axis=0, keepdims=True)


def final_call(w_piece, h_piece, *parts):
    rank, span = w_piece.shape
    return pl.pallas_call(
        final_kernel,
        in_specs=vmem(2 + len(parts)),
        out_specs=vmem(3),
        out_shape=[
            jax.ShapeDtypeStruct((rank, span), F32),
            jax.ShapeDtypeStruct(h_piece.shape, F32),
            jax.ShapeDtypeStruct((1, span), F32),
        ],
        compiler_params=params(),
        cost_estimate=cost(24 * rank * rank * span, 4 * rank * LANES * len(parts)),
        name="final_update",
    )(w_piece, h_piece, *parts)


def join_kernel(*refs):
    pieces, out, table = refs[:-2], refs[-2], refs[-1]
    width = pieces[0].shape[1]
    for index, piece in enumerate(pieces):
        table[index] = piece[...]
    me = lax.axis_index("mz")
    for index in range(len(pieces)):
        out[:, index * width : (index + 1) * width] = table[jnp.bitwise_xor(me, index)]


def join_call(*pieces):
    rank, width = pieces[0].shape
    return pl.pallas_call(
        join_kernel,
        in_specs=vmem(len(pieces)),
        out_specs=pl.BlockSpec(memory_space=pltpu.VMEM),
        out_shape=jax.ShapeDtypeStruct((rank, width * len(pieces)), F32),
        scratch_shapes=[pltpu.VMEM((len(pieces), rank, width), F32)],
        compiler_params=params(),
        cost_estimate=cost(0, 8 * rank * width * len(pieces)),
        name="join",
    )(*pieces)


def swap(value, axis, size, mask):
    return lax.ppermute(value, axis, [(i, i ^ mask) for i in range(size)])


def cross(value, groups, owners, even, odd):
    pairs = [
        (g * owners + o, (g ^ (even if o % 2 else odd)) * owners + o)
        for g in range(groups)
        for o in range(owners)
    ]
    return lax.ppermute(value, ("mz", "px"), pairs)


def spread(h_piece, owners, products):
    evens = [owners - 2, *range(2, owners - 2, 2)]
    mine = []
    for relative in evens:
        mine.append(swap(h_piece, "px", owners, relative))
    beside = swap(h_piece, "px", owners, 1)
    theirs = []
    for piece in mine:
        theirs.append(swap(piece, "px", owners, 1))
    total = products([0, 1], [h_piece, beside], None, False)
    total = products(evens, mine, total, False)
    return products([r + 1 for r in evens], theirs, total, True)


def fast_device(groups, owners, spectra, w_piece, h_piece):
    width = h_piece.shape[1]
    copy, high, low = split_call(spectra)
    pieces = [w_piece] * groups
    for k in range(1, groups):
        pieces[k] = swap(w_piece, "mz", groups, k)
    w_block = join_call(*pieces)
    evens = [owners - 2, *range(2, owners - 2, 2)]
    steps = [(1, 1)]
    if groups > 2:
        steps = [*[(k, k) for k in range(groups - 1, 2, -1)], (1, 2), (2, 1)]
    for iteration in range(ITERS):
        batches = [evens[:1], evens[1:]] if len(evens) > 1 else [evens]
        others = []
        for batch in batches:
            (theirs,) = scatter_call([r + 1 for r in batch], width, w_block, high, low)
            others.append(swap(theirs, "px", owners, 1))
        sent = []
        for batch, other in zip(batches, others):
            (own,) = scatter_call(batch, width, w_block, high, low)
            for relative, value in zip(batch, pair_call(own, other)):
                sent.append(swap(value, "px", owners, relative))
        beside, near = scatter_call([1, 0], width, w_block, high, low, False)
        beside = swap(beside, "px", owners, 1)
        h_piece = update_call(h_piece, near, beside, *sent)
        if iteration + 1 < ITERS:
            total = spread(
                h_piece,
                owners,
                lambda relatives, pieces, before, last: gather_call(relatives, pieces, high, low, before),
            )
            sent = []
            for even, odd in steps:
                sent.append(cross(total, groups, owners, even, odd))
            w_block = update_call(w_block, total, *sent)
        else:
            parts = spread(
                h_piece,
                owners,
                lambda relatives, pieces, before, last: final_gather_call(
                    relatives, groups, pieces, copy, w_block, before, last
                ),
            )
            sent = []
            for k in [*range(2, groups), 1]:
                sent.append(swap(parts[k], "mz", groups, k))
            w_final, h_final, misfit = final_call(parts[groups], h_piece, parts[0], *sent)
    return w_final, h_final, misfit.reshape(-1)


def per_device(groups, owners, spectra, w_piece, h_piece):
    rank = w_piece.shape[0]
    pixels, width = spectra.shape[0], h_piece.shape[1]

    def power(n):
        return n > 1 and n & (n - 1) == 0

    fits = (
        power(groups)
        and power(owners)
        and width % LANES == 0
        and pixels % LANES == 0
        and w_piece.shape[1] % SUBLANES == 0
        and rank % (2 * SUBLANES) == 0
        and rank // SUBLANES * rank <= min(width, pixels)
        and w_piece.shape[1] < LANES
        and LANES - w_piece.shape[1] < rank
        and (rank - LANES + w_piece.shape[1]) * (rank // SUBLANES) <= LANES
    )
    if fits:
        return fast_device(groups, owners, spectra, w_piece, h_piece)
    return plain_device(spectra, w_piece, h_piece)


def solution(mesh):
    in_specs = (P("px", "mz"), P(None, ("px", "mz")), P(None, ("mz", "px")))
    out_specs = (P(None, ("px", "mz")), P(None, ("mz", "px")), P(("px", "mz")))
    body = functools.partial(per_device, mesh.shape["mz"], mesh.shape["px"])
    return jax.shard_map(body, mesh=mesh, in_specs=in_specs, out_specs=out_specs, check_vma=False)
```

```python
import functools

import jax
import jax.numpy as jnp
from jax import lax
from jax.experimental import pallas as pl
from jax.experimental.pallas import tpu as pltpu
from jax.sharding import PartitionSpec as P


ITERS = 3
LANES = 128
SUBLANES = 8
F32 = jnp.float32
BF16 = jnp.bfloat16
NN = (((1,), (0,)), ((), ()))
NT = (((1,), (1,)), ((), ()))


def matmul(left, right):
    return jnp.dot(left, right, preferred_element_type=F32, precision=lax.Precision.HIGHEST)


def plain_device(spectra, w_piece, h_piece):
    def rows_of(piece):
        return lax.all_gather(piece, "mz", axis=1, tiled=True)

    w_block = rows_of(w_piece)
    for _ in range(ITERS):
        numerator = lax.psum_scatter(matmul(w_block, spectra), "px", scatter_dimension=1, tiled=True)
        gram_w = lax.psum(matmul(w_block, w_block.T), "px")
        h_piece = h_piece * numerator / matmul(gram_w, h_piece)
        h_block = lax.all_gather(h_piece, "px", axis=1, tiled=True)
        numerator = lax.psum_scatter(matmul(h_block, spectra.T), "mz", scatter_dimension=1, tiled=True)
        gram_h = lax.psum(matmul(h_block, h_block.T), "mz")
        w_piece = w_piece * numerator / matmul(gram_h, w_piece)
        w_block = rows_of(w_piece)
    difference = spectra - matmul(w_block.T, h_block)
    partial_error = jnp.sum(difference * difference, axis=1)
    misfit = lax.psum_scatter(partial_error, "mz", scatter_dimension=0, tiled=True)
    return (w_piece, h_piece, misfit)


def split(value):
    high = value.astype(BF16)
    return high, (value - high.astype(F32)).astype(BF16)


def exact(left, right, dims):
    return lax.dot_general(left, right, dims, precision=lax.Precision.HIGHEST, preferred_element_type=F32)


def fast(left, right, dims):
    return lax.dot_general(left, right, dims, preferred_element_type=F32)


def stacked(value):
    high, low = split(value)
    return jnp.concatenate([high, low], axis=0), high


def product(stack, high, s_high, s_low, dims):
    rows = high.shape[0]
    both = fast(stack, s_high, dims)
    return both[:rows] + both[rows:] + fast(high, s_low, dims)


def pack_gram(ref, gram):
    rank = gram.shape[0]
    ref[rank:, :] = jnp.zeros((SUBLANES, ref.shape[1]), F32)
    for group in range(rank // SUBLANES):
        rows = slice(group * SUBLANES, (group + 1) * SUBLANES)
        ref[rank:, group * rank : (group + 1) * rank] = gram[rows, :]


def unpack_gram(packed, rank):
    return jnp.concatenate(
        [packed[:, group * rank : (group + 1) * rank] for group in range(rank // SUBLANES)], axis=0
    )


def params(mib=32):
    return pltpu.CompilerParams(vmem_limit_bytes=mib << 20)


def vmem(count):
    return [pl.BlockSpec(memory_space=pltpu.VMEM)] * count


def cost(flops, moved):
    return pl.CostEstimate(flops=int(flops), bytes_accessed=int(moved), transcendentals=0)


def split_kernel(step, s_ref, copy_ref, high_ref, low_ref, sems):
    columns = s_ref.shape[1]
    copies = []
    for index in range(columns // step):
        here = pl.ds(index * step, step)
        copies.append(pltpu.make_async_copy(s_ref.at[:, here], copy_ref.at[:, here], sems.at[index]))
        copies[-1].start()
    for index, copy in enumerate(copies):
        here = pl.ds(index * step, step)
        copy.wait()
        high_ref[:, here], low_ref[:, here] = split(copy_ref[:, here])


def split_call(spectra):
    rows, columns = spectra.shape
    step = columns // 8 if columns % (8 * LANES) == 0 else columns
    return pl.pallas_call(
        functools.partial(split_kernel, step),
        in_specs=[pl.BlockSpec(memory_space=pltpu.HBM)],
        out_specs=vmem(3),
        out_shape=[
            jax.ShapeDtypeStruct((rows, columns), F32),
            jax.ShapeDtypeStruct((rows, columns), BF16),
            jax.ShapeDtypeStruct((rows, columns), BF16),
        ],
        scratch_shapes=[pltpu.SemaphoreType.DMA((columns // step,))],
        compiler_params=params(44),
        cost_estimate=cost(4 * rows * columns, 12 * rows * columns),
        name="split_spectra",
    )(spectra)


def bins_of(relative, width):
    block = jnp.bitwise_xor(lax.axis_index("px"), relative)
    return pl.ds(pl.multiple_of(block * width, LANES), width)


def scatter_kernel(relatives, width, w_ref, high_ref, low_ref, *outs):
    if len(outs[0].shape) == 3:
        outs = [outs[0].at[index] for index in range(len(relatives))]
    w = w_ref[...]
    rank = w.shape[0]
    stack, w_high = stacked(w)
    gram = product(stack, w_high, *split(w), NT)
    for relative, out in zip(relatives, outs):
        here = bins_of(relative, width)
        out[:rank, :] = product(stack, w_high, high_ref[:, here], low_ref[:, here], NN)
        pack_gram(out, gram)


def scatter_call(relatives, width, w_block, high, low, joined=True):
    rank, pixels = w_block.shape
    count = len(relatives)
    shape = (rank + SUBLANES, width)
    shapes = [(count, *shape)] if joined else [shape] * count
    return pl.pallas_call(
        functools.partial(scatter_kernel, relatives, width),
        in_specs=vmem(3),
        out_specs=vmem(len(shapes)),
        out_shape=[jax.ShapeDtypeStruct(shape, F32) for shape in shapes],
        compiler_params=params(),
        cost_estimate=cost(6 * rank * pixels * width * count, 4 * pixels * width * count),
        name="loadings_times_spectra",
    )(w_block, high, low)


def pair_kernel(own_ref, other_ref, *outs):
    for index, out in enumerate(outs):
        out[...] = own_ref[index] + other_ref[index]


def pair_call(own, other):
    count = own.shape[0]
    return pl.pallas_call(
        pair_kernel,
        in_specs=vmem(2),
        out_specs=vmem(count),
        out_shape=[jax.ShapeDtypeStruct(own.shape[1:], F32)] * count,
        compiler_params=params(),
        cost_estimate=cost(own.size, 12 * own.size),
        name="pair_sums",
    )(own, other)


def update_kernel(factor_ref, *refs):
    parts, out = refs[:-1], refs[-1]
    factor = factor_ref[...]
    rank = factor.shape[0]
    total = parts[0][...]
    for part in parts[1:]:
        total = total + part[...]
    gram = unpack_gram(total[rank:], rank)
    out[...] = factor * total[:rank] / exact(gram, factor, NN)


def update_call(factor, *parts):
    rank, width = factor.shape
    return pl.pallas_call(
        update_kernel,
        in_specs=vmem(1 + len(parts)),
        out_specs=pl.BlockSpec(memory_space=pltpu.VMEM),
        out_shape=jax.ShapeDtypeStruct((rank, width), F32),
        compiler_params=params(),
        cost_estimate=cost(12 * rank * rank * width, 4 * rank * width * (2 + len(parts))),
        name="update",
    )(factor, *parts)


def gather_kernel(relatives, carried, high_ref, low_ref, *refs):
    out = refs[-1]
    pieces = refs[: len(relatives)]
    rank, width = pieces[0].shape
    total, gram = None, None
    for relative, piece in zip(relatives, pieces):
        h = piece[...]
        stack, h_high = stacked(h)
        here = bins_of(relative, width)
        term = product(stack, h_high, high_ref[:, here], low_ref[:, here], NT)
        square = product(stack, h_high, *split(h), NT)
        total = term if total is None else total + term
        gram = square if gram is None else gram + square
    out[:rank, :] = total
    pack_gram(out, gram)
    if carried:
        out[...] += refs[len(relatives)][...]


def gather_call(relatives, pieces, high, low, before):
    rank, width = pieces[0].shape
    pixels = high.shape[0]
    extra = () if before is None else (before,)
    count = len(relatives)
    return pl.pallas_call(
        functools.partial(gather_kernel, relatives, before is not None),
        in_specs=vmem(2 + count + len(extra)),
        out_specs=pl.BlockSpec(memory_space=pltpu.VMEM),
        out_shape=jax.ShapeDtypeStruct((rank + SUBLANES, pixels), F32),
        compiler_params=params(),
        cost_estimate=cost(6 * rank * pixels * width * count, 4 * pixels * width * count),
        name="spectra_times_components",
    )(high, low, *pieces, *extra)


def thirds(value):
    high, low = split(value)
    return high, low, (value - high.astype(F32) - low.astype(F32)).astype(BF16)


def final_gather_kernel(relatives, groups, first, last, s_ref, w_ref, *refs):
    pieces, refs = refs[: len(relatives)], refs[len(relatives) :]
    carried, refs = ((), refs) if first else (refs[:3], refs[3:])
    rank, width = pieces[0].shape
    pixels = w_ref.shape[1]
    span = pixels // groups
    w = w_ref[...]
    w0, w1, w2 = thirds(w.T)
    left = jnp.concatenate([w0, w0, w1, w1, w2], axis=1)
    front = jnp.zeros((span, width), BF16)
    back = jnp.zeros((2 * LANES - span - rank, width), BF16)
    sums = [ref[...] for ref in carried] if carried else [None] * 3
    for relative, piece in zip(relatives, pieces):
        h0, h1 = split(piece[...])
        right = jnp.concatenate([h0, h1, h0, h1, h0], axis=0)
        d = s_ref[:, bins_of(relative, width)] - fast(left, right, NN)
        stack = jnp.concatenate([h0, h1], axis=0)
        error = product(stack, h0, *split(d), NT)
        gram = product(
            stack,
            h0,
            jnp.concatenate([front, h0, back], axis=0),
            jnp.concatenate([front, h1, back], axis=0),
            NT,
        )
        square = d * d
        folded = square[:, :LANES]
        for start in range(LANES, width, LANES):
            folded = folded + square[:, start : start + LANES]
        terms = (error, folded, gram)
        sums = [t if s is None else s + t for s, t in zip(sums, terms)]
    error, folded, gram = sums
    if not last:
        for ref, value in zip(refs, sums):
            ref[...] = value
        return
    outs, own_ref = refs[:groups], refs[groups]
    squares = exact(jnp.ones((SUBLANES, LANES), F32), folded, NT)
    table = jnp.concatenate([error, squares, w], axis=0)
    me = lax.axis_index("mz")
    free = LANES - span
    lane = lax.broadcasted_iota(jnp.int32, (rank, LANES), 1)
    for relative, out in enumerate(outs):
        group = jnp.bitwise_xor(me, relative)
        here = pltpu.roll(table, lax.rem(groups - group, groups) * span, 1)[:, :LANES]
        out[:rank, :] = jnp.where(lane < span, here[:rank], gram[:, :LANES])
        out[rank : rank + SUBLANES, :] = here[rank : rank + SUBLANES]
        out[rank + SUBLANES :, :] = jnp.zeros((SUBLANES, LANES), F32)
        rest = rank - free
        for index in range(rank // SUBLANES):
            rows = slice(index * SUBLANES, (index + 1) * SUBLANES)
            out[rank + SUBLANES :, index * rest : (index + 1) * rest] = gram[rows, LANES : LANES + rest]
        if relative == 0:
            own_ref[...] = here[rank + SUBLANES :, :span]


def final_gather_call(relatives, groups, pieces, spectra, w_block, before, last):
    rank, width = pieces[0].shape
    pixels = w_block.shape[1]
    count = len(relatives)
    first = before is None
    extra = () if first else tuple(before)
    shapes = [(rank, pixels), (pixels, LANES), (rank, 2 * LANES)]
    if last:
        shapes = [(rank + 2 * SUBLANES, LANES)] * groups + [(rank, pixels // groups)]
    return pl.pallas_call(
        functools.partial(final_gather_kernel, relatives, groups, first, last),
        in_specs=vmem(2 + count + len(extra)),
        out_specs=vmem(len(shapes)),
        out_shape=[jax.ShapeDtypeStruct(shape, F32) for shape in shapes],
        compiler_params=params(),
        cost_estimate=cost(18 * rank * pixels * width * count, 8 * pixels * width * count),
        name="final_products",
    )(spectra, w_block, *pieces, *extra)


def final_kernel(w_ref, h_ref, *refs):
    parts, (w_out, h_out, misfit_out) = refs[:-3], refs[-3:]
    h_out[...] = h_ref[...]
    w = w_ref[...]
    rank, span = w.shape
    total = parts[0][...]
    for part in parts[1:]:
        total = total + part[...]
    rest = rank - (LANES - span)
    low = total[rank + SUBLANES :]
    tail = [low[:, index * rest : (index + 1) * rest] for index in range(rank // SUBLANES)]
    gram = jnp.concatenate([total[:rank, span:], jnp.concatenate(tail, axis=0)], axis=1)
    error = total[:rank, :span]
    den = exact(gram, w, NN)
    new = w * (error + den) / den
    w_out[...] = new
    step = new - w
    change = step * (exact(gram, step, NN) - 2.0 * error)
    misfit_out[...] = total[rank : rank + 1, :span] + jnp.sum(change, axis=0, keepdims=True)


def final_call(w_piece, h_piece, *parts):
    rank, span = w_piece.shape
    return pl.pallas_call(
        final_kernel,
        in_specs=vmem(2 + len(parts)),
        out_specs=vmem(3),
        out_shape=[
            jax.ShapeDtypeStruct((rank, span), F32),
            jax.ShapeDtypeStruct(h_piece.shape, F32),
            jax.ShapeDtypeStruct((1, span), F32),
        ],
        compiler_params=params(),
        cost_estimate=cost(24 * rank * rank * span, 4 * rank * LANES * len(parts)),
        name="final_update",
    )(w_piece, h_piece, *parts)


def join_kernel(*refs):
    pieces, out, table = refs[:-2], refs[-2], refs[-1]
    width = pieces[0].shape[1]
    for index, piece in enumerate(pieces):
        table[index] = piece[...]
    me = lax.axis_index("mz")
    for index in range(len(pieces)):
        out[:, index * width : (index + 1) * width] = table[jnp.bitwise_xor(me, index)]


def join_call(*pieces):
    rank, width = pieces[0].shape
    return pl.pallas_call(
        join_kernel,
        in_specs=vmem(len(pieces)),
        out_specs=pl.BlockSpec(memory_space=pltpu.VMEM),
        out_shape=jax.ShapeDtypeStruct((rank, width * len(pieces)), F32),
        scratch_shapes=[pltpu.VMEM((len(pieces), rank, width), F32)],
        compiler_params=params(),
        cost_estimate=cost(0, 8 * rank * width * len(pieces)),
        name="join",
    )(*pieces)


def swap(value, axis, size, mask):
    return lax.ppermute(value, axis, [(i, i ^ mask) for i in range(size)])


def cross(value, groups, owners, even, odd):
    pairs = [
        (g * owners + o, (g ^ (even if o % 2 else odd)) * owners + o)
        for g in range(groups)
        for o in range(owners)
    ]
    return lax.ppermute(value, ("mz", "px"), pairs)


def spread(h_piece, owners, products, early=False):
    evens = [owners - 2, *range(2, owners - 2, 2)]
    mine = []
    for relative in evens:
        mine.append(swap(h_piece, "px", owners, relative))
    beside = swap(h_piece, "px", owners, 1)
    theirs = []
    for piece in mine:
        theirs.append(swap(piece, "px", owners, 1))
    total = products([0, 1], [h_piece, beside], None, False)
    if early:
        total = products(evens[:1], mine[:1], total, False)
        total = products(evens[1:], mine[1:], total, False)
    else:
        total = products(evens, mine, total, False)
    return products([r + 1 for r in evens], theirs, total, True)


def fast_device(groups, owners, spectra, w_piece, h_piece):
    width = h_piece.shape[1]
    copy, high, low = split_call(spectra)
    pieces = [w_piece] * groups
    for k in range(1, groups):
        pieces[k] = swap(w_piece, "mz", groups, k)
    w_block = join_call(*pieces)
    evens = [owners - 2, *range(2, owners - 2, 2)]
    steps = [(1, 1)]
    if groups > 2:
        steps = [*[(k, k) for k in range(groups - 1, 2, -1)], (1, 2), (2, 1)]
    for iteration in range(ITERS):
        batches = [evens[:1], evens[1:]] if len(evens) > 1 else [evens]
        others = []
        for batch in batches:
            (theirs,) = scatter_call([r + 1 for r in batch], width, w_block, high, low)
            others.append(swap(theirs, "px", owners, 1))
        sent = []
        for batch, other in zip(batches, others):
            (own,) = scatter_call(batch, width, w_block, high, low)
            for relative, value in zip(batch, pair_call(own, other)):
                sent.append(swap(value, "px", owners, relative))
        beside, near = scatter_call([1, 0], width, w_block, high, low, False)
        beside = swap(beside, "px", owners, 1)
        h_piece = update_call(h_piece, near, beside, *sent)
        if iteration + 1 < ITERS:
            total = spread(
                h_piece,
                owners,
                lambda relatives, pieces, before, last: gather_call(relatives, pieces, high, low, before),
            )
            sent = []
            for even, odd in steps:
                sent.append(cross(total, groups, owners, even, odd))
            w_block = update_call(w_block, total, *sent)
        else:
            parts = spread(
                h_piece,
                owners,
                lambda relatives, pieces, before, last: final_gather_call(
                    relatives, groups, pieces, copy, w_block, before, last
                ),
                True,
            )
            sent = []
            for k in [*range(2, groups), 1]:
                sent.append(swap(parts[k], "mz", groups, k))
            w_final, h_final, misfit = final_call(parts[groups], h_piece, parts[0], *sent)
    return w_final, h_final, misfit.reshape(-1)


def per_device(groups, owners, spectra, w_piece, h_piece):
    rank = w_piece.shape[0]
    pixels, width = spectra.shape[0], h_piece.shape[1]

    def power(n):
        return n > 1 and n & (n - 1) == 0

    fits = (
        power(groups)
        and power(owners)
        and width % LANES == 0
        and pixels % LANES == 0
        and w_piece.shape[1] % SUBLANES == 0
        and rank % (2 * SUBLANES) == 0
        and rank // SUBLANES * rank <= min(width, pixels)
        and w_piece.shape[1] < LANES
        and LANES - w_piece.shape[1] < rank
        and (rank - LANES + w_piece.shape[1]) * (rank // SUBLANES) <= LANES
    )
    if fits:
        return fast_device(groups, owners, spectra, w_piece, h_piece)
    return plain_device(spectra, w_piece, h_piece)


def solution(mesh):
    in_specs = (P("px", "mz"), P(None, ("px", "mz")), P(None, ("mz", "px")))
    out_specs = (P(None, ("px", "mz")), P(None, ("mz", "px")), P(("px", "mz")))
    body = functools.partial(per_device, mesh.shape["mz"], mesh.shape["px"])
    return jax.shard_map(body, mesh=mesh, in_specs=in_specs, out_specs=out_specs, check_vma=False)
```
